32 devices in a mesh: row: 16 (over z, x, core), col: 2 (over y).
Axes of the slice: x: 2, y: 2, z: 4, core: 2. Of those that a mesh axis runs over, the one named last changes fastest.
Arguments:
- x_train: bfloat16 [64, 8192], P(None, 'col'), may hold values from -8 to 8
- targets: float32 [8192], P('col'), may hold values from -6 to 6
- noise_draws: float32 [8192, 256], P('col', 'row'), may hold values from -3 to 3
- alpha_init: float32 [8192, 256], P('col', 'row'), may hold values from -6 to 6
- velocity_init: float32 [8192, 256], P('col', 'row'), may hold values from -3 to 3
- frequencies: bfloat16 [64, 4096], P(None, 'col'), may hold values from -5 to 5
- phases: float32 [4096], P('col'), may hold values from -3.140625 to 3.140625
- path_weights: bfloat16 [4096, 256], P('col'), may hold values from -6 to 6
- x_window: bfloat16 [64, 32768], P(None, 'row'), may hold values from -6 to 6
- batch_index: int32 [3, 8192], replicated, may hold values from 0 to 8191, as said below
Outputs:
- alpha_out: float32 [8192, 256], P('col', 'row')
- velocity_out: float32 [8192, 256], P('col', 'row')
- prior_window: float32 [256, 32768], P('col', 'row')
The draws below stay inside these ranges and needn't reach their ends.
Inputs may be any that keep to these rules, and one draw needn't show every extreme that they name: `batch_index`: row b of every step names a training point of group g = (b // 256) % 2, that is a number from g * 4096 to (g + 1) * 4096 - 1; points may repeat.
All inputs are finite; a program needn't handle non-finite values.
Results may differ from the reference program's by a relative error of at most 0.0039.
Values may be sent and summed in bfloat16 or wider, within the bound.
A program may use at most 64 MiB of HBM per device.

```python
import jax
import jax.numpy as jnp
from jax import lax

D_IN = 64
FEAT = 4096
PATHS = 256
STEPS = 3
TRAIN_DEV = 4096
BATCH_DEV = 512
WINDOW_DEV = 2048
TRAIN = 8192
BATCH = 8192
WINDOW = 32768
N_ROW = 16


def draw_x_train(key, part):
    clusters = max(TRAIN // 4, 1)
    center_scale = (40.0 / D_IN) ** 0.5
    offset_scale = (1.0 / D_IN) ** 0.5
    member = jax.random.randint(jax.random.fold_in(key, 14), (TRAIN,), 0, clusters)
    center_key = jax.random.fold_in(key, 15)
    offset_key = jax.random.fold_in(key, 16)
    centers = center_scale * jax.random.normal(center_key, (D_IN, clusters), jnp.float32)
    offsets = offset_scale * jax.random.normal(offset_key, (D_IN, TRAIN), jnp.float32)
    points = jnp.take(centers, member, axis=1) + offsets
    return jnp.clip(points, -8.0, 8.0).astype(jnp.bfloat16)


def draw_batch_index(key, part):
    col_groups = TRAIN // TRAIN_DEV
    own_rows = BATCH_DEV // col_groups
    positions = jnp.arange(BATCH)
    group_ids = positions // own_rows % col_groups
    offsets = jax.random.randint(jax.random.fold_in(key, 21), (STEPS, BATCH), 0, TRAIN_DEV)
    return (group_ids[None, :] * TRAIN_DEV + offsets).astype(jnp.int32)


def level_of(key, shape, cuts, smallest, top_value):
    loudness = 1.0
    for position, shards_of in cuts:
        steps = jax.random.uniform(jax.random.fold_in(jax.random.fold_in(key, 6), position), (shards_of,), jnp.float32, smallest / len(cuts), top_value / len(cuts))
        loudness = loudness * jnp.repeat(jnp.exp(steps), shape[position] // shards_of).reshape((-1,) + (1,) * (len(shape) - 1 - position))
    return loudness


def gaussian(rng, extent, deviation, most, pieces=(), kind=jnp.bfloat16):
    entries = deviation * jax.random.normal(rng, extent, jnp.float32)
    if pieces:
        entries = entries * level_of(rng, extent, pieces, -0.22, 0.18)
    return jnp.clip(entries, -most, most).astype(kind)


def setup_inputs(seed: int = 0) -> dict:
    key_list = jax.random.split(jax.random.key(seed), 11)
    x_train = draw_x_train(jax.random.fold_in(key_list[10], 71), 0)
    targets = gaussian(key_list[1], (TRAIN,), 1.0, 6.0, ((0, 2),), jnp.float32)
    noise_draws = gaussian(key_list[2], (TRAIN, PATHS), 0.5, 3.0, ((0, 2), (1, 16)), jnp.float32)
    alpha_init = gaussian(key_list[3], (TRAIN, PATHS), 1.0, 6.0, ((0, 2), (1, 16)), jnp.float32)
    velocity_init = gaussian(key_list[4], (TRAIN, PATHS), 0.5, 3.0, ((0, 2), (1, 16)), jnp.float32)
    frequencies = gaussian(key_list[5], (D_IN, FEAT), 0.87, 5.0, ((1, 2),))
    phases = jnp.clip(jax.random.uniform(key_list[6], (FEAT,), jnp.float32, -3.140625, 3.140625), -3.140625, 3.140625)
    path_weights = gaussian(key_list[7], (FEAT, PATHS), 1.0, 6.0, ((0, 2),))
    x_window = gaussian(key_list[8], (D_IN, WINDOW), 1.0, 6.0, ((1, 16),))
    batch_index = draw_batch_index(jax.random.fold_in(key_list[10], 71), 0)
    return dict(x_train=x_train, targets=targets, noise_draws=noise_draws, alpha_init=alpha_init, velocity_init=velocity_init, frequencies=frequencies, phases=phases, path_weights=path_weights, x_window=x_window, batch_index=batch_index)


SQRT_THREE = 1.7320508075688772
LENGTH = 1.15
NOISE_VAR = 0.25
MOMENTUM = 0.9
STEP_SIZE = 0.5
HIGH = lax.Precision.HIGHEST

def features(points, frequencies, phases):
    phase_arg = jnp.dot(frequencies.astype(jnp.float32).T, points.astype(jnp.float32), precision=HIGH)
    factor = (2.0 / FEAT) ** 0.5
    return (factor * jnp.cos(phase_arg + phases[:, None])).astype(jnp.bfloat16)

def kernel_rows(points, x_train, train_norm):
    inner_prod = jnp.dot(points.astype(jnp.float32).T, x_train.astype(jnp.float32), precision=HIGH)
    point_norm = lax.optimization_barrier(jnp.sum(jnp.square(points.astype(jnp.float32)), axis=0))
    dist_sq = jnp.maximum(point_norm[:, None] + train_norm[None, :] - 2.0 * inner_prod, 0.0)
    scaled = SQRT_THREE / LENGTH * jnp.sqrt(dist_sq)
    return ((1.0 + scaled) * jnp.exp(-scaled)).astype(jnp.bfloat16)

def reference(x_train, targets, noise_draws, alpha_init, velocity_init, frequencies, phases, path_weights, x_window, batch_index):
    weights_wide = path_weights.astype(jnp.float32)
    window_blocks = x_window.reshape(D_IN, N_ROW, WINDOW_DEV).transpose(1, 0, 2)

    def window_block(points):
        phi_block = lax.optimization_barrier(features(points, frequencies, phases)).astype(jnp.float32)
        return jnp.dot(weights_wide.T, phi_block, precision=HIGH)
    prior_blocks = lax.map(window_block, window_blocks)
    prior_window = prior_blocks.transpose(1, 0, 2).reshape(PATHS, WINDOW)
    train_norm = lax.optimization_barrier(jnp.sum(jnp.square(x_train.astype(jnp.float32)), axis=0))
    block_rows = min(256, BATCH)
    alpha = alpha_init
    velocity = velocity_init
    for step_id in range(STEPS):
        index_now = batch_index[step_id].astype(jnp.int32)
        points = jnp.take(x_train, index_now, axis=1)
        coeffs = lax.optimization_barrier(alpha.astype(jnp.bfloat16)).astype(jnp.float32)
        point_blocks = points.reshape(D_IN, BATCH // block_rows, block_rows).transpose(1, 0, 2)

        def batch_block(block_points):
            kernel = lax.optimization_barrier(kernel_rows(block_points, x_train, train_norm)).astype(jnp.float32)
            coupled = jnp.dot(kernel, coeffs, precision=HIGH)
            phi_block = lax.optimization_barrier(features(block_points, frequencies, phases)).astype(jnp.float32)
            return coupled + jnp.dot(phi_block.T, weights_wide, precision=HIGH)
        batch_sum = lax.map(batch_block, point_blocks).reshape(BATCH, PATHS)
        row_terms = batch_sum + NOISE_VAR * alpha[index_now] - targets[index_now][:, None] + noise_draws[index_now]
        gradient = jnp.zeros_like(alpha).at[index_now].add(row_terms)
        velocity = MOMENTUM * velocity - STEP_SIZE * gradient
        alpha = alpha + velocity
    return (alpha, velocity, prior_window)
```

```python
import functools

import jax
import jax.numpy as jnp
import numpy as np
from jax import lax
from jax.experimental import pallas as pl
from jax.experimental.pallas import tpu as pltpu
from jax.sharding import PartitionSpec as P

SQRT_THREE = 1.7320508075688772
LENGTH = 1.15
NOISE_VAR = 0.25
MOMENTUM = 0.9
STEP_SIZE = 0.5


def sine_coeffs(scale):
    nodes = 4
    k = np.arange(nodes)
    v = (np.cos((2 * k + 1) * np.pi / (2 * nodes)) + 1) / 2 / 16
    z = np.sqrt(v)
    q = np.sin(2 * np.pi * z) / z
    return [float(c * scale) for c in np.linalg.solve(np.vander(v, nodes, increasing=True), q)]


def scaled_cos(turns, coeffs):
    z = 0.25 - jnp.abs(turns - jnp.round(turns))
    v = z * z
    q = coeffs[-1]
    for c in coeffs[-2::-1]:
        q = q * v + c
    return q * z


def prior_kernel(coeffs, tile_f, freq_ref, phase_ref, weight_ref, point_ref, out_ref):
    feat = freq_ref.shape[0]
    points = point_ref[...]

    def body(i, acc):
        rows = pl.ds(pl.multiple_of(i * tile_f, tile_f), tile_f)
        arg = jnp.dot(freq_ref[rows, :], points, preferred_element_type=jnp.float32)
        turns = (arg + phase_ref[rows, :]) * (0.5 / np.pi)
        phi = scaled_cos(turns, coeffs).astype(jnp.bfloat16)
        return acc + lax.dot_general(
            weight_ref[rows, :], phi, (((0,), (0,)), ((), ())), preferred_element_type=jnp.float32
        )

    out_ref[...] = lax.fori_loop(0, feat // tile_f, body, jnp.zeros(out_ref.shape, jnp.float32))


def prior_sums(freq_t, phase_col, weights, points, total_feat):
    feat, d_in = freq_t.shape
    paths = weights.shape[1]
    n = points.shape[1]
    tile_n = min(512, n)
    coeffs = sine_coeffs((2.0 / total_feat) ** 0.5)
    return pl.pallas_call(
        functools.partial(prior_kernel, coeffs, min(256, feat)),
        grid=(n // tile_n,),
        in_specs=[
            pl.BlockSpec((feat, d_in), lambda i: (0, 0)),
            pl.BlockSpec((feat, 1), lambda i: (0, 0)),
            pl.BlockSpec((feat, paths), lambda i: (0, 0)),
            pl.BlockSpec((d_in, tile_n), lambda i: (0, i)),
        ],
        out_specs=pl.BlockSpec((paths, tile_n), lambda i: (0, i)),
        out_shape=jax.ShapeDtypeStruct((paths, n), jnp.float32),
        cost_estimate=pl.CostEstimate(
            flops=2 * feat * n * (paths + d_in), bytes_accessed=4 * paths * n, transcendentals=feat * n
        ),
    )(freq_t, phase_col, weights, points)


def matern(points, train):
    inner = lax.dot_general(
        train, points, (((0,), (0,)), ((), ())), preferred_element_type=jnp.float32
    )
    point_norm = jnp.sum(jnp.square(points.astype(jnp.float32)), axis=0)
    train_norm = jnp.sum(jnp.square(train.astype(jnp.float32)), axis=0)
    dist_sq = jnp.maximum(train_norm[:, None] + point_norm[None, :] - 2.0 * inner, 0.0)
    scaled = SQRT_THREE / LENGTH * jnp.sqrt(dist_sq)
    return ((1.0 + scaled) * jnp.exp(-scaled)).astype(jnp.bfloat16)


def point_counts(index, start, count):
    lanes = 128
    local = index - start
    high = (local // lanes)[:, None, :] == lax.broadcasted_iota(
        jnp.int32, (1, count // lanes, 1), 1
    )
    low = (local % lanes)[:, None, :] == lax.broadcasted_iota(jnp.int32, (1, lanes, 1), 1)
    tables = lax.dot_general(
        high.astype(jnp.bfloat16),
        low.astype(jnp.bfloat16),
        (((2,), (2,)), ((0,), (0,))),
        preferred_element_type=jnp.float32,
    )
    return tables.reshape(index.shape[0], count)


def shards(
    x_train,
    targets,
    noise_draws,
    alpha_init,
    velocity_init,
    frequencies,
    phases,
    path_weights,
    x_window,
    batch_index,
):
    row_count = lax.axis_size("row")
    col_count = lax.axis_size("col")
    row_id = lax.axis_index("row")
    col_id = lax.axis_index("col")
    train_cols = x_train.shape[1]
    own = train_cols // row_count
    steps = batch_index.shape[0]
    total_feat = frequencies.shape[1] * col_count

    mine = lax.dynamic_slice_in_dim(x_train, row_id * own, own, 1)
    points = lax.all_gather(mine, "col", axis=1, tiled=True)
    freq_t = frequencies.T
    phase_col = phases[:, None]
    kernel_tile = matern(points, x_train)
    prior_rows = prior_sums(freq_t, phase_col, path_weights, points, total_feat)
    window = prior_sums(freq_t, phase_col, path_weights, x_window, total_feat)
    prior_window = lax.psum_scatter(window, "col", scatter_dimension=0, tiled=True)

    counts = point_counts(batch_index, col_id * train_cols, train_cols)
    base = (noise_draws - targets[:, None]).T
    dual, velocity = alpha_init.T, velocity_init.T
    for step in range(steps):
        coeffs = lax.all_gather(dual.astype(jnp.bfloat16), "row", axis=0, tiled=True)
        sums = jnp.dot(coeffs, kernel_tile, preferred_element_type=jnp.float32) + prior_rows
        mine_sums = lax.psum_scatter(sums, "col", scatter_dimension=1, tiled=True)
        arrived = lax.all_to_all(mine_sums, "row", split_axis=0, concat_axis=1, tiled=True)
        gradient = counts[step][None, :] * (arrived + NOISE_VAR * dual + base)
        velocity = MOMENTUM * velocity - STEP_SIZE * gradient
        dual = dual + velocity
    return (dual.T, velocity.T, prior_window)


MESH = pl.DeviceIdType.MESH
TURN = 1.0 / (2.0 * np.pi)
DIST_SCALE = 3.0 / (LENGTH * LENGTH)


def split_three(value):
    parts = []
    for _ in range(3):
        part = value.astype(jnp.bfloat16).astype(jnp.float32)
        parts.append(part)
        value = value - part
    return parts


def tail_rows(rows, count, n):
    at = lax.broadcasted_iota(jnp.int32, (count, n), 0)
    tail = jnp.zeros((count, n), jnp.float32)
    for i, row in enumerate(rows):
        tail = jnp.where(at == i, row, tail)
    return tail


DIMS = "yxz"
LOADS = (
    "alpha", "x", "index", "target", "noise", "velocity", "freq", "phase", "weight", "window",
)
PIECES = ((0, 256, "yxz"), (256, 256, "yzx"))
MASKS = ("y", "x", "z", "yx", "yz", "xz", "yxz")


def mask_of(dims):
    return "".join(d for d in DIMS if d in dims)


def fused_kernel(
    scale_coeffs, steps, rows, pieces, x_hbm, target_hbm, noise_hbm, alpha_hbm, velocity_hbm,
    freq_hbm, phase_hbm, weight_hbm, window_hbm, index_hbm, alpha_ref, velocity_ref, prior_ref,
    x_ref, target_ref, noise_ref, alpha_in, velocity_in, freq_ref, phase_ref, weight_ref,
    window_ref, index_ref, load_sem,
    gathered, tile, train_aug, window_aug, point_aug, freq_t, weight_t, phi_buf, acc,
    pull_a, pull_v, prior_t, prior_out, prior_in, count_ref, count_t, x_in, start_out, start_in, entry_out, entry_in,
    exit_out, exit_in, window_acc, window_out, window_in,
    hop_send, hop_recv, pair_send, pair_recv, entry_send, entry_recv, exit_send, exit_recv,
    misc_send, misc_recv,
):
    div, rem = lax.div, lax.rem
    f32, bf16 = jnp.float32, jnp.bfloat16
    row = lax.axis_index("row")
    col = lax.axis_index("col")
    peer = 1 - col
    devices = rows * 2
    paths = weight_ref.shape[1]
    share = paths // rows
    kept = paths // 2
    train = x_ref.shape[1]
    team = rows // 2
    own = train // team
    feat = freq_ref.shape[1]
    d_in = x_ref.shape[0]
    window = window_ref.shape[1]
    core = rem(row, 2)
    group = div(row, team)
    local = rem(row, team)
    flip = {"x": 2 - 4 * rem(div(row, 2), 2), "z": 4 - 8 * rem(div(row, 4), 2)}
    sibling = row + 1 - 2 * core
    block = 256

    def at(start, size, unit=None):
        return pl.ds(pl.multiple_of(start, unit or size), size)

    def mate(d):
        return rem(local + d + 1, team)

    def remote(src, dst, send, recv, device):
        return pltpu.make_async_remote_copy(
            src_ref=src, dst_ref=dst, send_sem=send, recv_sem=recv,
            device_id=device, device_id_type=MESH,
        )

    def loop(n, action):
        def one(i, carry):
            action(i)
            return carry

        lax.fori_loop(0, n, one, 0)

    def load(name):
        i = LOADS.index(name)
        src, dst = (
            (alpha_hbm, alpha_in), (x_hbm, x_ref), (index_hbm, index_ref),
            (target_hbm, target_ref), (noise_hbm, noise_ref), (velocity_hbm, velocity_in),
            (freq_hbm, freq_ref), (phase_hbm, phase_ref), (weight_hbm, weight_ref),
            (window_hbm, window_ref),
        )[i]
        return pltpu.make_async_copy(src, dst, load_sem.at[i])

    def loaded(*names):
        for name in names:
            load(name).wait()

    barrier = pltpu.get_barrier_semaphore()
    pl.semaphore_signal(barrier, inc=1, device_id=(row, peer), device_id_type=MESH)
    loop(team - 1, lambda d: pl.semaphore_signal(
        barrier, inc=1, device_id=(group * team + mate(d), col), device_id_type=MESH
    ))
    for name in LOADS:
        load(name).start()

    def source(mask):
        r = row
        for d in "xz":
            r = r + flip[d] if d in mask else r
        return r, (peer if "y" in mask else col)

    def first_row(r, c):
        return (c * team + rem(r, team)) * own

    def piece(step, mask, q, twin=False):
        r, c = source(mask)
        r = r + 1 - 2 * core if twin else r
        start, size, _ = pieces[q]
        return gathered.at[step, at(first_row(r, c) + start, size, 16), :]

    def hop(step, mask, d, q):
        ref = piece(step, mask, q)
        i = MASKS.index(mask_of(mask + d))
        return remote(
            ref, ref, hop_send.at[step, q, i], hop_recv.at[step, q, i], source(d)
        )

    def arrival(step, mask, q):
        ref = piece(step, mask, q)
        i = MASKS.index(mask)
        return remote(ref, ref, hop_send.at[step, q, i], hop_recv.at[step, q, i], (sibling, col))

    def pair(step, mask, q, twin=False):
        ref = piece(step, mask, q, twin)
        i = MASKS.index(mask) + 1 if mask else 0
        return remote(
            ref, ref, pair_send.at[step, q, i], pair_recv.at[step, q, i], (sibling, col)
        )

    count = range(len(pieces))

    def start_gather(step):
        for place in range(3):
            for q in count:
                hop(step, "", pieces[q][2][place], q).start()
        for q in count:
            pair(step, "", q).start()

    def relay(step, which):
        for q in count:
            order = pieces[q][2]
            mask = mask_of([order[i] for i in which])
            arrival(step, mask, q).wait_recv()
            for d in order[max(which) + 1 :]:
                hop(step, mask, d, q).start()
            pair(step, mask, q).start()

    def product(step, masks):
        for mask in masks:
            for q in count:
                pair(step, mask, q, True).wait_recv()
        wide = 2 * len(masks)
        r, c = source(masks[0])
        first = (c * team + div(rem(r, team), wide) * wide) * own
        span = at(first, wide * own)
        return dot(tile[:, span], gathered[step, span, :])

    def x_copy():
        half = train // 2
        cols = at(core * half, half)
        return remote(
            x_ref.at[:, cols], x_in.at[:, cols], misc_send.at[0], misc_recv.at[0], (row, peer)
        )

    def x_pair():
        half = train // 2
        ref = x_in.at[:, at(core * half, half)]
        return remote(ref, ref, misc_send.at[1], misc_recv.at[1], (sibling, col))

    def x_twin():
        half = train // 2
        ref = x_in.at[:, at((1 - core) * half, half)]
        return remote(ref, ref, misc_send.at[1], misc_recv.at[1], (sibling, col))

    def prior_copy():
        return remote(prior_out, prior_in, misc_send.at[2], misc_recv.at[2], (row, peer))

    parts = window_out.shape[0]

    def window_copy(part):
        return remote(
            window_out.at[part], window_in.at[part],
            misc_send.at[3 + part], misc_recv.at[3 + part], (row, peer),
        )

    def entry_refs(kind):
        if kind == 0:
            return start_out, start_in
        return entry_out.at[kind - 1], entry_in.at[kind - 1]

    def entry_copy(kind, d):
        m = mate(d)
        out, into = entry_refs(kind)
        return remote(
            out.at[:, at(m * own, own)], into.at[at(local * share, share), :],
            entry_send.at[kind, m], entry_recv.at[kind, local], (group * team + m, col),
        )

    def entry_arrival(kind, d):
        m = mate(d)
        out, into = entry_refs(kind)
        return remote(
            out.at[:, at(m * own, own)], into.at[at(m * share, share), :],
            entry_send.at[kind, m], entry_recv.at[kind, m], (group * team + m, col),
        )

    def send_entry(kind, value):
        out, into = entry_refs(kind)
        if kind:
            out[...] = value
        loop(team - 1, lambda d: entry_copy(kind, d).start())
        into[at(local * share, share), :] = out[:, at(local * own, own)]

    def take_entry(kind):
        loop(team - 1, lambda d: entry_arrival(kind, d).wait_recv())
        return entry_refs(kind)[1][...].astype(f32).T

    def exit_copy(kind, d):
        m = mate(d)
        return remote(
            exit_out.at[kind, at(m * share, share), :],
            exit_in.at[kind, :, at(local * own, own)],
            exit_send.at[kind, m], exit_recv.at[kind, local], (group * team + m, col),
        )

    def exit_arrival(kind, d):
        m = mate(d)
        return remote(
            exit_out.at[kind, at(m * share, share), :],
            exit_in.at[kind, :, at(m * own, own)],
            exit_send.at[kind, m], exit_recv.at[kind, m], (group * team + m, col),
        )

    def send_exit(kind, value):
        exit_out[kind] = value.T.astype(bf16)
        loop(team - 1, lambda d: exit_copy(kind, d).start())
        exit_in[kind, :, at(local * own, own)] = exit_out[kind, at(local * share, share), :]

    def take_exit(kind):
        loop(team - 1, lambda d: exit_arrival(kind, d).wait_recv())
        return exit_in[kind].astype(f32)

    def dot(a, b):
        return jnp.dot(a, b, preferred_element_type=f32)

    def against(a, b):
        return lax.dot_general(a, b, (((1,), (1,)), ((), ())), preferred_element_type=f32)

    def add_train(ref, c):
        def one(i):
            x = ref[:, at(i * block, block)]
            cols = at(c * train + i * block, block)
            for part in range(3):
                train_aug[part * d_in : (part + 1) * d_in, cols] = x
            norm = DIST_SCALE * jnp.sum(jnp.square(x.astype(f32)), axis=0, keepdims=True)
            tail = tail_rows([1.0, 1.0, 1.0] + split_three(norm), 16, block)
            train_aug[3 * d_in : 3 * d_in + 16, cols] = tail.astype(bf16)
            train_aug[3 * d_in + 16 :, cols] = jnp.zeros((d_in - 16, block), bf16)

        loop(train // block, one)

    def add_points():
        for i in range(own // block):
            x = x_ref[:, at(local * own + i * block, block)].astype(f32)
            norm = DIST_SCALE * jnp.sum(jnp.square(x), axis=0, keepdims=True)
            tail = tail_rows(split_three(norm) + [1.0, 1.0, 1.0], d_in, block)
            stack = jnp.concatenate(split_three(-2.0 * DIST_SCALE * x) + [tail], axis=0)
            point_aug[i * block : (i + 1) * block, :] = stack.T.astype(bf16)

    def add_window():
        for part in range(3):
            window_aug[part * d_in : (part + 1) * d_in, :] = window_ref[...]
        window_aug[3 * d_in :, :] = tail_rows([1.0] * 3, d_in, window).astype(bf16)

    def add_freq():
        def one(i):
            cols = at(i * block, block)
            tail = tail_rows(split_three(phase_ref[:, cols] * TURN), d_in, block)
            stack = jnp.concatenate(
                split_three(freq_ref[:, cols].astype(f32) * TURN) + [tail], axis=0
            )
            freq_t[cols, :] = stack.T.astype(bf16)
            weight_t[:, cols] = weight_ref[cols, :].astype(f32).T.astype(bf16)

        loop(feat // block, one)

    def count_points(step):
        lanes = 128
        width = index_ref.shape[1] // devices
        index = jnp.concatenate(
            [index_ref[step : step + 1, at((2 * i + col) * width, width)] for i in range(rows)],
            axis=1,
        )
        index = index - col * train
        high_ids = lax.broadcasted_iota(jnp.int32, (train // lanes, 1), 0)
        low_ids = lax.broadcasted_iota(jnp.int32, (lanes, 1), 0)
        high = ((index >> 7) == high_ids).astype(f32).astype(bf16)
        low = ((index & 127) == low_ids).astype(f32).astype(bf16)
        table = against(high, low)
        for i in range(train // lanes):
            count_ref[step : step + 1, i * lanes : (i + 1) * lanes] = table[i : i + 1, :]

    def spread_counts():
        for step in range(steps):
            line = count_ref[step : step + 1, at(local * own, own)]
            count_t[step] = jnp.broadcast_to(line, (kept, own)).T

    def fill_phi(rhs, first, n):
        width = 512

        def one(i):
            turns = dot(freq_t[at(first + i * width, width), :], rhs)
            phi_buf[at(i * width, width), :] = scaled_cos(turns, scale_coeffs).astype(bf16)

        loop(n // width, one)

    def prior_points(c, out):
        def one(i):
            fill_phi(train_aug[:, at(c * train + local * own + i * block, block)], 0, feat)
            out[at(i * block, block), :] = dot(weight_t[at(group * kept, kept), :], phi_buf[...]).T

        loop(own // block, one)

    def fill_tile(i):
        cols = at(i * block, block)
        dist_sq = jnp.maximum(dot(point_aug[...], train_aug[:, cols]), 1e-30)
        scaled = dist_sq * lax.rsqrt(dist_sq)
        tile[:, cols] = ((1.0 + scaled) * jnp.exp(-scaled)).astype(bf16)

    tiles = train // block

    def fill_tiles(c, first, n):
        loop(n, lambda i: fill_tile(c * tiles + first + i))

    def window_work(i, f):
        half = feat // 2
        span = at(i * block, block)
        fill_phi(window_aug[:, span], f * half, half)
        sums = dot(weight_t[:, at(f * half, half)], phi_buf[:half, :])
        if f == 0:
            window_acc[...] = sums
            return
        total = window_acc[...] + sums
        prior_ref[:, span] = jnp.where(col == 0, total[:kept], total[kept:])
        per = window // block // parts
        window_out[i // per, :, (i % per) * block : (i % per + 1) * block] = jnp.where(
            col == 0, total[kept:], total[:kept]
        ).astype(bf16)
        if i % per == per - 1:
            window_copy(i // per).start()

    loaded("alpha")
    start_out[...] = alpha_in[...].astype(bf16)
    pl.semaphore_wait(barrier, team)
    send_entry(0, None)
    loaded("x")
    x_copy().start()
    loaded("index")
    for step in range(steps):
        count_points(step)
    loaded("target", "noise", "velocity")
    base = noise_ref[...] - target_ref[...]
    speed = velocity_in[...]
    free = alpha_in[...]
    for step in range(steps):
        speed = MOMENTUM * speed - STEP_SIZE * (
            count_ref[step : step + 1, :] * (NOISE_VAR * free + base)
        )
        if step < steps - 1:
            free = free + speed
            send_entry(1 + step, free)
    alpha_ref[...] = free
    velocity_ref[...] = speed
    add_train(x_ref, col)
    add_points()
    fill_tiles(col, 0, 4)
    gathered[0, at(first_row(row, col), own), :] = take_entry(0).astype(bf16)
    start_gather(0)
    loaded("freq", "phase", "weight")
    add_freq()
    fill_tiles(col, 4, tiles - 4)
    relay(0, (0,))
    relay(0, (1,))
    relay(0, (2,))
    x_copy().wait_recv()
    x_pair().start()
    prior_points(col, prior_t)
    relay(0, (0, 1))
    x_twin().wait_recv()
    add_train(x_in, peer)
    prior_points(peer, prior_out)
    prior_copy().start()
    relay(0, (0, 2))
    relay(0, (1, 2))
    fill_tiles(peer, 0, tiles // 2)
    relay(0, (0, 1, 2))
    fill_tiles(peer, tiles // 2, tiles // 2)
    spread_counts()
    loaded("window")
    add_window()
    for mask in ("",) + MASKS:
        for q in count:
            pair(0, mask, q, True).wait_recv()
    acc[...] = dot(tile[...], gathered[0])
    prior_copy().wait_recv()
    prior_t[...] += prior_in[...]

    for step in range(1, steps + 1):
        sums = acc[...] + prior_t[...]
        if step == 1:
            speed = -STEP_SIZE * (count_t[0] * sums)
            pull = speed
        else:
            pull = pull_a[...]
            speed = MOMENTUM * pull_v[...] - STEP_SIZE * (
                count_t[step - 1] * (sums + NOISE_VAR * pull)
            )
            pull = pull + speed
        if step == steps:
            send_exit(1, speed)
            break
        pull_v[...] = speed
        pull_a[...] = pull
        gathered[step, at(first_row(row, col), own), :] = (take_entry(step) + pull).astype(bf16)
        start_gather(step)
        chunks = window // block // (steps - 1)
        work = [
            (lambda i, f: lambda: window_work(i, f))((step - 1) * chunks + i, f)
            for i in range(chunks) for f in (0, 1)
        ]

        def run(n):
            for _ in range(n):
                work.pop(0)()

        run(3)
        relay(step, (0,))
        relay(step, (1,))
        relay(step, (2,))
        run(2)
        relay(step, (0, 1))
        acc[...] = product(step, ("", "x"))
        run(1)
        relay(step, (0, 2))
        relay(step, (1, 2))
        if step == steps - 1:
            send_exit(0, pull_a[...])
        run(len(work))
        acc[...] += product(step, ("y", "yx"))
        relay(step, (0, 1, 2))
        acc[...] += product(step, ("z", "xz"))
        acc[...] += product(step, ("yz",))
        acc[...] += product(step, ("yxz",))

    alpha_ref[...] += take_exit(0)
    for part in range(parts):
        window_copy(part).wait()
        width = window // parts
        span = slice(part * width, (part + 1) * width)
        prior_ref[:, span] = prior_ref[:, span] + window_in[part].astype(f32)
    speed = velocity_ref[...] + take_exit(1)
    velocity_ref[...] = speed
    alpha_ref[...] += speed
    x_copy().wait_send()
    x_pair().wait_send()
    prior_copy().wait_send()
    for kind in range(steps):
        loop(team - 1, lambda d: entry_copy(kind, d).wait_send())
    for kind in range(2):
        loop(team - 1, lambda d: exit_copy(kind, d).wait_send())
    for step in range(steps):
        for q in count:
            for mask in MASKS:
                arrival(step, mask, q).wait_send()
                pair(step, mask, q).wait_send()
            pair(step, "", q).wait_send()


def fused_shards(
    x_train, targets, noise_draws, alpha_init, velocity_init, frequencies, phases, path_weights,
    x_window, batch_index,
):
    rows = lax.axis_size("row")
    col_count = lax.axis_size("col")
    d_in, train = x_train.shape
    steps = batch_index.shape[0]
    feat, paths = path_weights.shape
    share = paths // rows
    own = 2 * train // rows
    kept = paths // 2
    window = x_window.shape[1]
    parts = 4
    coeffs = sine_coeffs((2.0 / (feat * col_count)) ** 0.5)
    vmem = pl.BlockSpec(memory_space=pltpu.VMEM)
    dma = pltpu.SemaphoreType.DMA
    f32, bf16 = jnp.float32, jnp.bfloat16
    n = len(PIECES)
    alpha, velocity, prior = pl.pallas_call(
        functools.partial(fused_kernel, coeffs, steps, rows, PIECES),
        in_specs=[pl.BlockSpec(memory_space=pltpu.HBM)] * 10,
        out_specs=[vmem] * 3,
        out_shape=(
            jax.ShapeDtypeStruct((share, train), f32),
            jax.ShapeDtypeStruct((share, train), f32),
            jax.ShapeDtypeStruct((kept, window), f32),
        ),
        scratch_shapes=[
            pltpu.VMEM((d_in, train), bf16),
            pltpu.VMEM((1, train), f32),
            pltpu.VMEM((share, train), f32),
            pltpu.VMEM((share, train), f32),
            pltpu.VMEM((share, train), f32),
            pltpu.VMEM((d_in, feat), bf16),
            pltpu.VMEM((1, feat), f32),
            pltpu.VMEM((feat, paths), bf16),
            pltpu.VMEM((d_in, window), bf16),
            pltpu.VMEM(batch_index.shape, jnp.int32),
            dma((10,)),
            pltpu.VMEM((steps, 2 * train, kept), bf16),
            pltpu.VMEM((own, 2 * train), bf16),
            pltpu.VMEM((4 * d_in, 2 * train), bf16),
            pltpu.VMEM((4 * d_in, window), bf16),
            pltpu.VMEM((own, 4 * d_in), bf16),
            pltpu.VMEM((feat, 4 * d_in), bf16),
            pltpu.VMEM((paths, feat), bf16),
            pltpu.VMEM((feat, 256), bf16),
            pltpu.VMEM((own, kept), f32),
            pltpu.VMEM((own, kept), f32),
            pltpu.VMEM((own, kept), f32),
            pltpu.VMEM((own, kept), f32),
            pltpu.VMEM((own, kept), f32),
            pltpu.VMEM((own, kept), f32),
            pltpu.VMEM((steps, train), f32),
            pltpu.VMEM((steps, own, kept), f32),
            pltpu.VMEM((d_in, train), bf16),
            pltpu.VMEM((share, train), bf16),
            pltpu.VMEM((kept, own), bf16),
            pltpu.VMEM((steps - 1, share, train), f32),
            pltpu.VMEM((steps - 1, kept, own), f32),
            pltpu.VMEM((2, kept, own), bf16),
            pltpu.VMEM((2, share, train), bf16),
            pltpu.VMEM((paths, 256), f32),
            pltpu.VMEM((parts, kept, window // parts), bf16),
            pltpu.VMEM((parts, kept, window // parts), bf16),
            dma((steps, n, 7)), dma((steps, n, 7)), dma((steps, n, 8)), dma((steps, n, 8)),
            dma((steps, rows // 2)), dma((steps, rows // 2)),
            dma((2, rows // 2)), dma((2, rows // 2)),
            dma((3 + parts,)), dma((3 + parts,)),
        ],
        compiler_params=pltpu.CompilerParams(
            collective_id=0, has_side_effects=True, vmem_limit_bytes=44 * 1024 * 1024
        ),
    )(
        *(pltpu.with_memory_space_constraint(a, pltpu.HBM) for a in (
            x_train, targets[None, :], noise_draws.T, alpha_init.T, velocity_init.T, frequencies,
            phases[None, :], path_weights, x_window, batch_index,
        ))
    )
    return alpha.T, velocity.T, prior


def fits(mesh, args):
    x_train, batch_index, path_weights, x_window = args[0], args[9], args[7], args[8]
    rows = mesh.shape["row"]
    d_in, train = x_train.shape
    feat, paths = path_weights.shape
    return (
        mesh.shape["col"] == 2 and rows == 16 and d_in == 64 and train == 256 * rows
        and paths == 16 * rows and feat % 1024 == 0 and x_window.shape[1] == 2048
        and batch_index.shape[0] == 3 and batch_index.shape[1] % (256 * rows) == 0
    )


def solution(mesh):
    def body(*args):
        return (fused_shards if fits(mesh, args) else shards)(*args)

    placed = (
        P(None, "col"),
        P("col"),
        P("col", "row"),
        P("col", "row"),
        P("col", "row"),
        P(None, "col"),
        P("col"),
        P("col", None),
        P(None, "row"),
        P(),
    )
    return jax.shard_map(
        body,
        mesh=mesh,
        in_specs=placed,
        out_specs=(P("col", "row"), P("col", "row"), P("col", "row")),
        check_vma=False,
    )
```

```python
import functools

import jax
import jax.numpy as jnp
import numpy as np
from jax import lax
from jax.experimental import pallas as pl
from jax.experimental.pallas import tpu as pltpu
from jax.sharding import PartitionSpec as P

SQRT_THREE = 1.7320508075688772
LENGTH = 1.15
NOISE_VAR = 0.25
MOMENTUM = 0.9
STEP_SIZE = 0.5


def sine_coeffs(scale):
    nodes = 4
    k = np.arange(nodes)
    v = (np.cos((2 * k + 1) * np.pi / (2 * nodes)) + 1) / 2 / 16
    z = np.sqrt(v)
    q = np.sin(2 * np.pi * z) / z
    return [float(c * scale) for c in np.linalg.solve(np.vander(v, nodes, increasing=True), q)]


def scaled_cos(turns, coeffs):
    z = 0.25 - jnp.abs(turns - jnp.round(turns))
    v = z * z
    q = coeffs[-1]
    for c in coeffs[-2::-1]:
        q = q * v + c
    return q * z


def prior_kernel(coeffs, tile_f, freq_ref, phase_ref, weight_ref, point_ref, out_ref):
    feat = freq_ref.shape[0]
    points = point_ref[...]

    def body(i, acc):
        rows = pl.ds(pl.multiple_of(i * tile_f, tile_f), tile_f)
        arg = jnp.dot(freq_ref[rows, :], points, preferred_element_type=jnp.float32)
        turns = (arg + phase_ref[rows, :]) * (0.5 / np.pi)
        phi = scaled_cos(turns, coeffs).astype(jnp.bfloat16)
        return acc + lax.dot_general(
            weight_ref[rows, :], phi, (((0,), (0,)), ((), ())), preferred_element_type=jnp.float32
        )

    out_ref[...] = lax.fori_loop(0, feat // tile_f, body, jnp.zeros(out_ref.shape, jnp.float32))


def prior_sums(freq_t, phase_col, weights, points, total_feat):
    feat, d_in = freq_t.shape
    paths = weights.shape[1]
    n = points.shape[1]
    tile_n = min(512, n)
    coeffs = sine_coeffs((2.0 / total_feat) ** 0.5)
    return pl.pallas_call(
        functools.partial(prior_kernel, coeffs, min(256, feat)),
        grid=(n // tile_n,),
        in_specs=[
            pl.BlockSpec((feat, d_in), lambda i: (0, 0)),
            pl.BlockSpec((feat, 1), lambda i: (0, 0)),
            pl.BlockSpec((feat, paths), lambda i: (0, 0)),
            pl.BlockSpec((d_in, tile_n), lambda i: (0, i)),
        ],
        out_specs=pl.BlockSpec((paths, tile_n), lambda i: (0, i)),
        out_shape=jax.ShapeDtypeStruct((paths, n), jnp.float32),
        cost_estimate=pl.CostEstimate(
            flops=2 * feat * n * (paths + d_in), bytes_accessed=4 * paths * n, transcendentals=feat * n
        ),
    )(freq_t, phase_col, weights, points)


def matern(points, train):
    inner = lax.dot_general(
        train, points, (((0,), (0,)), ((), ())), preferred_element_type=jnp.float32
    )
    point_norm = jnp.sum(jnp.square(points.astype(jnp.float32)), axis=0)
    train_norm = jnp.sum(jnp.square(train.astype(jnp.float32)), axis=0)
    dist_sq = jnp.maximum(train_norm[:, None] + point_norm[None, :] - 2.0 * inner, 0.0)
    scaled = SQRT_THREE / LENGTH * jnp.sqrt(dist_sq)
    return ((1.0 + scaled) * jnp.exp(-scaled)).astype(jnp.bfloat16)


def point_counts(index, start, count):
    lanes = 128
    local = index - start
    high = (local // lanes)[:, None, :] == lax.broadcasted_iota(
        jnp.int32, (1, count // lanes, 1), 1
    )
    low = (local % lanes)[:, None, :] == lax.broadcasted_iota(jnp.int32, (1, lanes, 1), 1)
    tables = lax.dot_general(
        high.astype(jnp.bfloat16),
        low.astype(jnp.bfloat16),
        (((2,), (2,)), ((0,), (0,))),
        preferred_element_type=jnp.float32,
    )
    return tables.reshape(index.shape[0], count)


def shards(
    x_train,
    targets,
    noise_draws,
    alpha_init,
    velocity_init,
    frequencies,
    phases,
    path_weights,
    x_window,
    batch_index,
):
    row_count = lax.axis_size("row")
    col_count = lax.axis_size("col")
    row_id = lax.axis_index("row")
    col_id = lax.axis_index("col")
    train_cols = x_train.shape[1]
    own = train_cols // row_count
    steps = batch_index.shape[0]
    total_feat = frequencies.shape[1] * col_count

    mine = lax.dynamic_slice_in_dim(x_train, row_id * own, own, 1)
    points = lax.all_gather(mine, "col", axis=1, tiled=True)
    freq_t = frequencies.T
    phase_col = phases[:, None]
    kernel_tile = matern(points, x_train)
    prior_rows = prior_sums(freq_t, phase_col, path_weights, points, total_feat)
    window = prior_sums(freq_t, phase_col, path_weights, x_window, total_feat)
    prior_window = lax.psum_scatter(window, "col", scatter_dimension=0, tiled=True)

    counts = point_counts(batch_index, col_id * train_cols, train_cols)
    base = (noise_draws - targets[:, None]).T
    dual, velocity = alpha_init.T, velocity_init.T
    for step in range(steps):
        coeffs = lax.all_gather(dual.astype(jnp.bfloat16), "row", axis=0, tiled=True)
        sums = jnp.dot(coeffs, kernel_tile, preferred_element_type=jnp.float32) + prior_rows
        mine_sums = lax.psum_scatter(sums, "col", scatter_dimension=1, tiled=True)
        arrived = lax.all_to_all(mine_sums, "row", split_axis=0, concat_axis=1, tiled=True)
        gradient = counts[step][None, :] * (arrived + NOISE_VAR * dual + base)
        velocity = MOMENTUM * velocity - STEP_SIZE * gradient
        dual = dual + velocity
    return (dual.T, velocity.T, prior_window)


MESH = pl.DeviceIdType.MESH
TURN = 1.0 / (2.0 * np.pi)
DIST_SCALE = 3.0 / (LENGTH * LENGTH)


def split_three(value):
    parts = []
    for _ in range(3):
        part = value.astype(jnp.bfloat16).astype(jnp.float32)
        parts.append(part)
        value = value - part
    return parts


def tail_rows(rows, count, n):
    at = lax.broadcasted_iota(jnp.int32, (count, n), 0)
    tail = jnp.zeros((count, n), jnp.float32)
    for i, row in enumerate(rows):
        tail = jnp.where(at == i, row, tail)
    return tail


DIMS = "yxz"
LOADS = (
    "alpha", "x", "index", "target", "noise", "velocity", "freq", "phase", "weight", "window",
)
PIECES = ((0, 128, "yxz"), (128, 128, "yzx"), (256, 128, "yxz"), (384, 128, "yzx"))
MASKS = ("y", "x", "z", "yx", "yz", "xz", "yxz")


def mask_of(dims):
    return "".join(d for d in DIMS if d in dims)


def fused_kernel(
    scale_coeffs, steps, rows, pieces, x_hbm, target_hbm, noise_hbm, alpha_hbm, velocity_hbm,
    freq_hbm, phase_hbm, weight_hbm, window_hbm, index_hbm, alpha_ref, velocity_ref, prior_ref,
    x_ref, target_ref, noise_ref, alpha_in, velocity_in, freq_ref, phase_ref, weight_ref,
    window_ref, index_ref, load_sem,
    gathered, tile, train_aug, window_aug, point_aug, freq_t, weight_t, phi_buf, acc,
    pull_a, pull_v, prior_t, prior_out, prior_in, count_ref, count_t, x_in, start_out, start_in, entry_out, entry_in,
    exit_out, exit_in, window_out, window_in,
    hop_send, hop_recv, pair_send, pair_recv, entry_send, entry_recv, exit_send, exit_recv,
    misc_send, misc_recv, x_send, x_recv,
):
    div, rem = lax.div, lax.rem
    f32, bf16 = jnp.float32, jnp.bfloat16
    row = lax.axis_index("row")
    col = lax.axis_index("col")
    peer = 1 - col
    devices = rows * 2
    paths = weight_ref.shape[1]
    share = paths // rows
    kept = paths // 2
    train = x_ref.shape[1]
    team = rows // 2
    own = train // team
    feat = freq_ref.shape[1]
    d_in = x_ref.shape[0]
    window = window_ref.shape[1]
    core = rem(row, 2)
    group = div(row, team)
    local = rem(row, team)
    flip = {"x": 2 - 4 * rem(div(row, 2), 2), "z": 4 - 8 * rem(div(row, 4), 2)}
    sibling = row + 1 - 2 * core
    block = 256

    def at(start, size, unit=None):
        return pl.ds(pl.multiple_of(start, unit or size), size)

    def mate(d):
        return rem(local + d + 1, team)

    def remote(src, dst, send, recv, device):
        return pltpu.make_async_remote_copy(
            src_ref=src, dst_ref=dst, send_sem=send, recv_sem=recv,
            device_id=device, device_id_type=MESH,
        )

    def loop(n, action):
        def one(i, carry):
            action(i)
            return carry

        lax.fori_loop(0, n, one, 0)

    def load(name):
        i = LOADS.index(name)
        src, dst = (
            (alpha_hbm, alpha_in), (x_hbm, x_ref), (index_hbm, index_ref),
            (target_hbm, target_ref), (noise_hbm, noise_ref), (velocity_hbm, velocity_in),
            (freq_hbm, freq_ref), (phase_hbm, phase_ref), (weight_hbm, weight_ref),
            (window_hbm, window_ref),
        )[i]
        return pltpu.make_async_copy(src, dst, load_sem.at[i])

    def loaded(*names):
        for name in names:
            load(name).wait()

    barrier = pltpu.get_barrier_semaphore()
    pl.semaphore_signal(barrier, inc=1, device_id=(row, peer), device_id_type=MESH)
    loop(team - 1, lambda d: pl.semaphore_signal(
        barrier, inc=1, device_id=(group * team + mate(d), col), device_id_type=MESH
    ))
    for name in LOADS:
        load(name).start()

    def source(mask):
        r = row
        for d in "xz":
            r = r + flip[d] if d in mask else r
        return r, (peer if "y" in mask else col)

    def first_row(r, c):
        return (c * team + rem(r, team)) * own

    def piece(step, mask, q, twin=False):
        r, c = source(mask)
        r = r + 1 - 2 * core if twin else r
        start, size, _ = pieces[q]
        return gathered.at[step, at(first_row(r, c) + start, size, 16), :]

    def hop(step, mask, d, q):
        ref = piece(step, mask, q)
        i = MASKS.index(mask_of(mask + d))
        return remote(
            ref, ref, hop_send.at[step, q, i], hop_recv.at[step, q, i], source(d)
        )

    def arrival(step, mask, q):
        ref = piece(step, mask, q)
        i = MASKS.index(mask)
        return remote(ref, ref, hop_send.at[step, q, i], hop_recv.at[step, q, i], (sibling, col))

    def pair(step, mask, q, twin=False):
        ref = piece(step, mask, q, twin)
        i = MASKS.index(mask) + 1 if mask else 0
        return remote(
            ref, ref, pair_send.at[step, q, i], pair_recv.at[step, q, i], (sibling, col)
        )

    count = range(len(pieces))

    def start_gather(step):
        for place in range(3):
            for q in count:
                hop(step, "", pieces[q][2][place], q).start()
        for q in count:
            pair(step, "", q).start()

    def relay(step, which, ahead=None):
        for q in count:
            order = pieces[q][2]
            mask = mask_of([order[i] for i in which])
            arrival(step, mask, q).wait_recv()
            for d in order[max(which) + 1 : ahead]:
                hop(step, mask, d, q).start()
            pair(step, mask, q).start()

    def relay_first(step):
        relay(step, (0,), 2)
        for q in count:
            order = pieces[q][2]
            hop(step, order[0], order[2], q).start()
        relay(step, (1,))
        relay(step, (2,))

    def product(step, masks):
        for mask in masks:
            for q in count:
                pair(step, mask, q, True).wait_recv()
        wide = 2 * len(masks)
        r, c = source(masks[0])
        first = (c * team + div(rem(r, team), wide) * wide) * own
        span = at(first, wide * own)
        return dot(tile[:, span], gathered[step, span, :])

    def x_span(on_core, part):
        width = train // 4
        return at((on_core * 2 + part) * width, width)

    def x_copy(part):
        cols = x_span(core, part)
        return remote(
            x_ref.at[:, cols], x_in.at[:, cols], x_send.at[0, part], x_recv.at[0, part],
            (row, peer),
        )

    def x_pair(part, twin=False):
        ref = x_in.at[:, x_span(1 - core if twin else core, part)]
        return remote(ref, ref, x_send.at[1, part], x_recv.at[1, part], (sibling, col))

    def prior_copy():
        return remote(prior_out, prior_in, misc_send.at[2], misc_recv.at[2], (row, peer))

    parts = window_out.shape[0]

    def window_copy(part):
        return remote(
            window_out.at[part], window_in.at[part],
            misc_send.at[3 + part], misc_recv.at[3 + part], (row, peer),
        )

    def entry_refs(kind):
        if kind == 0:
            return start_out, start_in
        return entry_out.at[kind - 1], entry_in.at[kind - 1]

    def entry_copy(kind, d):
        m = mate(d)
        out, into = entry_refs(kind)
        return remote(
            out.at[:, at(m * own, own)], into.at[at(local * share, share), :],
            entry_send.at[kind, m], entry_recv.at[kind, local], (group * team + m, col),
        )

    def entry_arrival(kind, d):
        m = mate(d)
        out, into = entry_refs(kind)
        return remote(
            out.at[:, at(m * own, own)], into.at[at(m * share, share), :],
            entry_send.at[kind, m], entry_recv.at[kind, m], (group * team + m, col),
        )

    def send_entry(kind, value):
        out, into = entry_refs(kind)
        if kind:
            out[...] = value
        loop(team - 1, lambda d: entry_copy(kind, d).start())
        into[at(local * share, share), :] = out[:, at(local * own, own)]

    def take_entry(kind):
        loop(team - 1, lambda d: entry_arrival(kind, d).wait_recv())
        return entry_refs(kind)[1][...].astype(f32).T

    def exit_copy(kind, d):
        m = mate(d)
        return remote(
            exit_out.at[kind, at(m * share, share), :],
            exit_in.at[kind, :, at(local * own, own)],
            exit_send.at[kind, m], exit_recv.at[kind, local], (group * team + m, col),
        )

    def exit_arrival(kind, d):
        m = mate(d)
        return remote(
            exit_out.at[kind, at(m * share, share), :],
            exit_in.at[kind, :, at(m * own, own)],
            exit_send.at[kind, m], exit_recv.at[kind, m], (group * team + m, col),
        )

    def send_exit(kind, value):
        exit_out[kind] = value.T.astype(bf16)
        loop(team - 1, lambda d: exit_copy(kind, d).start())
        exit_in[kind, :, at(local * own, own)] = exit_out[kind, at(local * share, share), :]

    def take_exit(kind):
        loop(team - 1, lambda d: exit_arrival(kind, d).wait_recv())
        return exit_in[kind].astype(f32)

    def dot(a, b):
        return jnp.dot(a, b, preferred_element_type=f32)

    def against(a, b):
        return lax.dot_general(a, b, (((1,), (1,)), ((), ())), preferred_element_type=f32)

    def add_train(ref, c):
        def one(i):
            x = ref[:, at(i * block, block)]
            cols = at(c * train + i * block, block)
            for part in range(3):
                train_aug[part * d_in : (part + 1) * d_in, cols] = x
            norm = DIST_SCALE * jnp.sum(jnp.square(x.astype(f32)), axis=0, keepdims=True)
            tail = tail_rows([1.0, 1.0, 1.0] + split_three(norm), 16, block)
            train_aug[3 * d_in : 3 * d_in + 16, cols] = tail.astype(bf16)
            train_aug[3 * d_in + 16 :, cols] = jnp.zeros((d_in - 16, block), bf16)

        loop(train // block, one)

    def add_points():
        for i in range(own // block):
            x = x_ref[:, at(local * own + i * block, block)].astype(f32)
            norm = DIST_SCALE * jnp.sum(jnp.square(x), axis=0, keepdims=True)
            tail = tail_rows(split_three(norm) + [1.0, 1.0, 1.0], d_in, block)
            stack = jnp.concatenate(split_three(-2.0 * DIST_SCALE * x) + [tail], axis=0)
            point_aug[i * block : (i + 1) * block, :] = stack.T.astype(bf16)

    def add_window():
        for part in range(3):
            window_aug[part * d_in : (part + 1) * d_in, :] = window_ref[...]
        window_aug[3 * d_in :, :] = tail_rows([1.0] * 3, d_in, window).astype(bf16)

    def add_freq():
        def one(i):
            cols = at(i * block, block)
            tail = tail_rows(split_three(phase_ref[:, cols] * TURN), d_in, block)
            stack = jnp.concatenate(
                split_three(freq_ref[:, cols].astype(f32) * TURN) + [tail], axis=0
            )
            freq_t[cols, :] = stack.T.astype(bf16)
            weight_t[:, cols] = weight_ref[cols, :].astype(f32).T.astype(bf16)

        loop(feat // block, one)

    def count_points(step):
        lanes = 128
        width = index_ref.shape[1] // devices
        index = jnp.concatenate(
            [index_ref[step : step + 1, at((2 * i + col) * width, width)] for i in range(rows)],
            axis=1,
        )
        index = index - col * train
        high_ids = lax.broadcasted_iota(jnp.int32, (train // lanes, 1), 0)
        low_ids = lax.broadcasted_iota(jnp.int32, (lanes, 1), 0)
        high = ((index >> 7) == high_ids).astype(f32).astype(bf16)
        low = ((index & 127) == low_ids).astype(f32).astype(bf16)
        table = against(high, low)
        for i in range(train // lanes):
            count_ref[step : step + 1, i * lanes : (i + 1) * lanes] = table[i : i + 1, :]

    def spread_counts(step):
        line = count_ref[step : step + 1, at(local * own, own)]
        count_t[step] = jnp.broadcast_to(line, (kept, own)).T

    def sums_over_features(rhs, weights):
        phi_buf[...] = scaled_cos(dot(freq_t[...], rhs), scale_coeffs).astype(bf16)
        return dot(weights, phi_buf[...])

    def prior_points(c, out):
        rhs = train_aug[:, at(c * train + local * own, own)]
        out[...] = sums_over_features(rhs, weight_t[at(group * kept, kept), :]).T

    def fill_tile(i):
        for part in range(2):
            cols = at(i * 4 * block + part * 2 * block, 2 * block)
            for half in range(2):
                span = slice(half * own // 2, (half + 1) * own // 2)
                dist_sq = jnp.maximum(dot(point_aug[span, :], train_aug[:, cols]), 1e-30)
                scaled = dist_sq * lax.rsqrt(dist_sq)
                tile[span, cols] = ((1.0 + scaled) * jnp.exp(-scaled)).astype(bf16)

    tiles = train // (4 * block)

    def fill_tiles(c, first, n):
        loop(n, lambda i: fill_tile(c * tiles + first + i))

    def window_work(i):
        width = window // parts
        span = slice(i * width, (i + 1) * width)
        total = sums_over_features(window_aug[:, span], weight_t[...])
        prior_ref[:, span] = jnp.where(col == 0, total[:kept], total[kept:])
        window_out[i] = jnp.where(col == 0, total[kept:], total[:kept]).astype(bf16)
        window_copy(i).start()

    loaded("alpha")
    start_out[...] = alpha_in[...].astype(bf16)
    pl.semaphore_wait(barrier, team)
    send_entry(0, None)
    loaded("x")
    x_copy(0).start()
    add_train(x_ref, col)
    add_points()
    fill_tiles(col, 0, 1)
    loaded("index")
    count_points(0)
    gathered[0, at(first_row(row, col), own), :] = take_entry(0).astype(bf16)
    start_gather(0)
    x_copy(1).start()
    loaded("freq", "phase", "weight")
    add_freq()
    fill_tiles(col, 1, tiles - 1)
    count_points(1)
    relay_first(0)
    x_copy(0).wait_recv()
    x_pair(0).start()
    prior_points(col, prior_t)
    x_copy(1).wait_recv()
    x_pair(1).start()
    for step in range(steps - 1):
        spread_counts(step)
    loaded("window")
    add_window()
    relay(0, (0, 1))
    for part in (0, 1):
        x_pair(part, True).wait_recv()
    add_train(x_in, peer)
    prior_points(peer, prior_out)
    prior_copy().start()
    relay(0, (0, 2))
    relay(0, (1, 2))
    loaded("target", "noise", "velocity")
    base = noise_ref[...] - target_ref[...]
    speed = velocity_in[...]
    free = alpha_in[...]
    for step in range(steps - 1):
        speed = MOMENTUM * speed - STEP_SIZE * (
            count_ref[step : step + 1, :] * (NOISE_VAR * free + base)
        )
        free = free + speed
        send_entry(1 + step, free)
    alpha_ref[...] = free
    velocity_ref[...] = speed
    fill_tiles(peer, 0, tiles // 2)
    relay(0, (0, 1, 2))
    fill_tiles(peer, tiles // 2, tiles // 2)
    for mask in ("",) + MASKS:
        for q in count:
            pair(0, mask, q, True).wait_recv()
    acc[...] = dot(tile[...], gathered[0])
    prior_copy().wait_recv()
    prior_t[...] += prior_in[...]

    for step in range(1, steps + 1):
        sums = acc[...] + prior_t[...]
        if step == 1:
            speed = -STEP_SIZE * (count_t[0] * sums)
            pull = speed
        else:
            pull = pull_a[...]
            speed = MOMENTUM * pull_v[...] - STEP_SIZE * (
                count_t[step - 1] * (sums + NOISE_VAR * pull)
            )
            pull = pull + speed
        if step == steps:
            send_exit(1, speed)
            break
        pull_v[...] = speed
        pull_a[...] = pull
        gathered[step, at(first_row(row, col), own), :] = (take_entry(step) + pull).astype(bf16)
        start_gather(step)
        chunks = parts // (steps - 1)
        first = (step - 1) * chunks
        window_work(first)
        relay_first(step)
        acc[...] = product(step, ("", "x"))
        if step == 1:
            count_points(steps - 1)
            spread_counts(steps - 1)
        relay(step, (0, 1))
        for i in range(1, chunks):
            window_work(first + i)
        if step == 1:
            final = count_ref[steps - 1 : steps, :]
            base = noise_ref[...] - target_ref[...]
            velocity_ref[...] = MOMENTUM * velocity_ref[...] - STEP_SIZE * (
                final * (NOISE_VAR * alpha_ref[...] + base)
            )
        relay(step, (0, 2))
        relay(step, (1, 2))
        if step == steps - 1:
            send_exit(0, pull_a[...])
        acc[...] += product(step, ("y", "yx"))
        relay(step, (0, 1, 2))
        acc[...] += product(step, ("z", "xz"))
        acc[...] += product(step, ("yz",))
        acc[...] += product(step, ("yxz",))

    alpha_ref[...] += take_exit(0)
    for part in range(parts):
        window_copy(part).wait()
        width = window // parts
        span = slice(part * width, (part + 1) * width)
        prior_ref[:, span] = prior_ref[:, span] + window_in[part].astype(f32)
    speed = velocity_ref[...] + take_exit(1)
    velocity_ref[...] = speed
    alpha_ref[...] += speed
    for part in (0, 1):
        x_copy(part).wait_send()
        x_pair(part).wait_send()
    prior_copy().wait_send()
    for kind in range(steps):
        loop(team - 1, lambda d: entry_copy(kind, d).wait_send())
    for kind in range(2):
        loop(team - 1, lambda d: exit_copy(kind, d).wait_send())
    for step in range(steps):
        for q in count:
            for mask in MASKS:
                arrival(step, mask, q).wait_send()
                pair(step, mask, q).wait_send()
            pair(step, "", q).wait_send()


def fused_shards(
    x_train, targets, noise_draws, alpha_init, velocity_init, frequencies, phases, path_weights,
    x_window, batch_index,
):
    rows = lax.axis_size("row")
    col_count = lax.axis_size("col")
    d_in, train = x_train.shape
    steps = batch_index.shape[0]
    feat, paths = path_weights.shape
    share = paths // rows
    own = 2 * train // rows
    kept = paths // 2
    window = x_window.shape[1]
    parts = 4
    coeffs = sine_coeffs((2.0 / (feat * col_count)) ** 0.5)
    vmem = pl.BlockSpec(memory_space=pltpu.VMEM)
    dma = pltpu.SemaphoreType.DMA
    f32, bf16 = jnp.float32, jnp.bfloat16
    n = len(PIECES)
    alpha, velocity, prior = pl.pallas_call(
        functools.partial(fused_kernel, coeffs, steps, rows, PIECES),
        in_specs=[pl.BlockSpec(memory_space=pltpu.HBM)] * 10,
        out_specs=[vmem] * 3,
        out_shape=(
            jax.ShapeDtypeStruct((share, train), f32),
            jax.ShapeDtypeStruct((share, train), f32),
            jax.ShapeDtypeStruct((kept, window), f32),
        ),
        scratch_shapes=[
            pltpu.VMEM((d_in, train), bf16),
            pltpu.VMEM((1, train), f32),
            pltpu.VMEM((share, train), f32),
            pltpu.VMEM((share, train), f32),
            pltpu.VMEM((share, train), f32),
            pltpu.VMEM((d_in, feat), bf16),
            pltpu.VMEM((1, feat), f32),
            pltpu.VMEM((feat, paths), bf16),
            pltpu.VMEM((d_in, window), bf16),
            pltpu.VMEM(batch_index.shape, jnp.int32),
            dma((10,)),
            pltpu.VMEM((steps, 2 * train, kept), bf16),
            pltpu.VMEM((own, 2 * train), bf16),
            pltpu.VMEM((4 * d_in, 2 * train), bf16),
            pltpu.VMEM((4 * d_in, window), bf16),
            pltpu.VMEM((own, 4 * d_in), bf16),
            pltpu.VMEM((feat, 4 * d_in), bf16),
            pltpu.VMEM((paths, feat), bf16),
            pltpu.VMEM((feat, own), bf16),
            pltpu.VMEM((own, kept), f32),
            pltpu.VMEM((own, kept), f32),
            pltpu.VMEM((own, kept), f32),
            pltpu.VMEM((own, kept), f32),
            pltpu.VMEM((own, kept), f32),
            pltpu.VMEM((own, kept), f32),
            pltpu.VMEM((steps, train), f32),
            pltpu.VMEM((steps, own, kept), f32),
            pltpu.VMEM((d_in, train), bf16),
            pltpu.VMEM((share, train), bf16),
            pltpu.VMEM((kept, own), bf16),
            pltpu.VMEM((steps - 1, share, train), f32),
            pltpu.VMEM((steps - 1, kept, own), f32),
            pltpu.VMEM((2, kept, own), bf16),
            pltpu.VMEM((2, share, train), bf16),
            pltpu.VMEM((parts, kept, window // parts), bf16),
            pltpu.VMEM((parts, kept, window // parts), bf16),
            dma((steps, n, 7)), dma((steps, n, 7)), dma((steps, n, 8)), dma((steps, n, 8)),
            dma((steps, rows // 2)), dma((steps, rows // 2)),
            dma((2, rows // 2)), dma((2, rows // 2)),
            dma((3 + parts,)), dma((3 + parts,)), dma((2, 2)), dma((2, 2)),
        ],
        compiler_params=pltpu.CompilerParams(
            collective_id=0, has_side_effects=True, vmem_limit_bytes=44 * 1024 * 1024
        ),
    )(
        *(pltpu.with_memory_space_constraint(a, pltpu.HBM) for a in (
            x_train, targets[None, :], noise_draws.T, alpha_init.T, velocity_init.T, frequencies,
            phases[None, :], path_weights, x_window, batch_index,
        ))
    )
    return alpha.T, velocity.T, prior


def fits(mesh, args):
    x_train, batch_index, path_weights, x_window = args[0], args[9], args[7], args[8]
    rows = mesh.shape["row"]
    d_in, train = x_train.shape
    feat, paths = path_weights.shape
    return (
        mesh.shape["col"] == 2 and rows == 16 and d_in == 64 and train == 256 * rows
        and paths == 16 * rows and feat % 1024 == 0 and x_window.shape[1] == 2048
        and batch_index.shape[0] == 3 and batch_index.shape[1] % (256 * rows) == 0
    )


def solution(mesh):
    def body(*args):
        return (fused_shards if fits(mesh, args) else shards)(*args)

    placed = (
        P(None, "col"),
        P("col"),
        P("col", "row"),
        P("col", "row"),
        P("col", "row"),
        P(None, "col"),
        P("col"),
        P("col", None),
        P(None, "row"),
        P(),
    )
    return jax.shard_map(
        body,
        mesh=mesh,
        in_specs=placed,
        out_specs=(P("col", "row"), P("col", "row"), P("col", "row")),
        check_vma=False,
    )
```

```python
import functools

import jax
import jax.numpy as jnp
import numpy as np
from jax import lax
from jax.experimental import pallas as pl
from jax.experimental.pallas import tpu as pltpu
from jax.sharding import PartitionSpec as P

SQRT_THREE = 1.7320508075688772
LENGTH = 1.15
NOISE_VAR = 0.25
MOMENTUM = 0.9
STEP_SIZE = 0.5


def sine_coeffs(scale):
    nodes = 4
    k = np.arange(nodes)
    v = (np.cos((2 * k + 1) * np.pi / (2 * nodes)) + 1) / 2 / 16
    z = np.sqrt(v)
    q = np.sin(2 * np.pi * z) / z
    return [float(c * scale) for c in np.linalg.solve(np.vander(v, nodes, increasing=True), q)]


def scaled_cos(turns, coeffs):
    z = 0.25 - jnp.abs(turns - jnp.round(turns))
    v = z * z
    q = coeffs[-1]
    for c in coeffs[-2::-1]:
        q = q * v + c
    return q * z


def prior_kernel(coeffs, tile_f, freq_ref, phase_ref, weight_ref, point_ref, out_ref):
    feat = freq_ref.shape[0]
    points = point_ref[...]

    def body(i, acc):
        rows = pl.ds(pl.multiple_of(i * tile_f, tile_f), tile_f)
        arg = jnp.dot(freq_ref[rows, :], points, preferred_element_type=jnp.float32)
        turns = (arg + phase_ref[rows, :]) * (0.5 / np.pi)
        phi = scaled_cos(turns, coeffs).astype(jnp.bfloat16)
        return acc + lax.dot_general(
            weight_ref[rows, :], phi, (((0,), (0,)), ((), ())), preferred_element_type=jnp.float32
        )

    out_ref[...] = lax.fori_loop(0, feat // tile_f, body, jnp.zeros(out_ref.shape, jnp.float32))


def prior_sums(freq_t, phase_col, weights, points, total_feat):
    feat, d_in = freq_t.shape
    paths = weights.shape[1]
    n = points.shape[1]
    tile_n = min(512, n)
    coeffs = sine_coeffs((2.0 / total_feat) ** 0.5)
    return pl.pallas_call(
        functools.partial(prior_kernel, coeffs, min(256, feat)),
        grid=(n // tile_n,),
        in_specs=[
            pl.BlockSpec((feat, d_in), lambda i: (0, 0)),
            pl.BlockSpec((feat, 1), lambda i: (0, 0)),
            pl.BlockSpec((feat, paths), lambda i: (0, 0)),
            pl.BlockSpec((d_in, tile_n), lambda i: (0, i)),
        ],
        out_specs=pl.BlockSpec((paths, tile_n), lambda i: (0, i)),
        out_shape=jax.ShapeDtypeStruct((paths, n), jnp.float32),
        cost_estimate=pl.CostEstimate(
            flops=2 * feat * n * (paths + d_in), bytes_accessed=4 * paths * n, transcendentals=feat * n
        ),
    )(freq_t, phase_col, weights, points)


def matern(points, train):
    inner = lax.dot_general(
        train, points, (((0,), (0,)), ((), ())), preferred_element_type=jnp.float32
    )
    point_norm = jnp.sum(jnp.square(points.astype(jnp.float32)), axis=0)
    train_norm = jnp.sum(jnp.square(train.astype(jnp.float32)), axis=0)
    dist_sq = jnp.maximum(train_norm[:, None] + point_norm[None, :] - 2.0 * inner, 0.0)
    scaled = SQRT_THREE / LENGTH * jnp.sqrt(dist_sq)
    return ((1.0 + scaled) * jnp.exp(-scaled)).astype(jnp.bfloat16)


def point_counts(index, start, count):
    lanes = 128
    local = index - start
    high = (local // lanes)[:, None, :] == lax.broadcasted_iota(
        jnp.int32, (1, count // lanes, 1), 1
    )
    low = (local % lanes)[:, None, :] == lax.broadcasted_iota(jnp.int32, (1, lanes, 1), 1)
    tables = lax.dot_general(
        high.astype(jnp.bfloat16),
        low.astype(jnp.bfloat16),
        (((2,), (2,)), ((0,), (0,))),
        preferred_element_type=jnp.float32,
    )
    return tables.reshape(index.shape[0], count)


def shards(
    x_train,
    targets,
    noise_draws,
    alpha_init,
    velocity_init,
    frequencies,
    phases,
    path_weights,
    x_window,
    batch_index,
):
    row_count = lax.axis_size("row")
    col_count = lax.axis_size("col")
    row_id = lax.axis_index("row")
    col_id = lax.axis_index("col")
    train_cols = x_train.shape[1]
    own = train_cols // row_count
    steps = batch_index.shape[0]
    total_feat = frequencies.shape[1] * col_count

    mine = lax.dynamic_slice_in_dim(x_train, row_id * own, own, 1)
    points = lax.all_gather(mine, "col", axis=1, tiled=True)
    freq_t = frequencies.T
    phase_col = phases[:, None]
    kernel_tile = matern(points, x_train)
    prior_rows = prior_sums(freq_t, phase_col, path_weights, points, total_feat)
    window = prior_sums(freq_t, phase_col, path_weights, x_window, total_feat)
    prior_window = lax.psum_scatter(window, "col", scatter_dimension=0, tiled=True)

    counts = point_counts(batch_index, col_id * train_cols, train_cols)
    base = (noise_draws - targets[:, None]).T
    dual, velocity = alpha_init.T, velocity_init.T
    for step in range(steps):
        coeffs = lax.all_gather(dual.astype(jnp.bfloat16), "row", axis=0, tiled=True)
        sums = jnp.dot(coeffs, kernel_tile, preferred_element_type=jnp.float32) + prior_rows
        mine_sums = lax.psum_scatter(sums, "col", scatter_dimension=1, tiled=True)
        arrived = lax.all_to_all(mine_sums, "row", split_axis=0, concat_axis=1, tiled=True)
        gradient = counts[step][None, :] * (arrived + NOISE_VAR * dual + base)
        velocity = MOMENTUM * velocity - STEP_SIZE * gradient
        dual = dual + velocity
    return (dual.T, velocity.T, prior_window)


MESH = pl.DeviceIdType.MESH
TURN = 1.0 / (2.0 * np.pi)
DIST_SCALE = 3.0 / (LENGTH * LENGTH)


def split_three(value):
    parts = []
    for _ in range(3):
        part = value.astype(jnp.bfloat16).astype(jnp.float32)
        parts.append(part)
        value = value - part
    return parts


def tail_rows(rows, count, n):
    at = lax.broadcasted_iota(jnp.int32, (count, n), 0)
    tail = jnp.zeros((count, n), jnp.float32)
    for i, row in enumerate(rows):
        tail = jnp.where(at == i, row, tail)
    return tail


DIMS = "yxz"
LOADS = (
    "alpha", "x", "index", "target", "noise", "velocity", "freq", "phase", "weight", "window",
)
PIECES = ((0, 128, "yxz"), (128, 128, "yzx"), (256, 128, "yxz"), (384, 128, "yzx"))
MASKS = ("y", "x", "z", "yx", "yz", "xz", "yxz")


def mask_of(dims):
    return "".join(d for d in DIMS if d in dims)


def fused_kernel(
    scale_coeffs, steps, rows, pieces, x_hbm, target_hbm, noise_hbm, alpha_hbm, velocity_hbm,
    freq_hbm, phase_hbm, weight_hbm, window_hbm, index_hbm, alpha_ref, velocity_ref, prior_ref,
    x_ref, target_ref, noise_ref, alpha_in, velocity_in, freq_ref, phase_ref, weight_ref,
    window_ref, index_ref, load_sem,
    gathered, tile, train_aug, window_aug, point_aug, freq_t, weight_t, phi_buf, acc,
    pull_a, pull_v, prior_t, prior_out, prior_in, count_ref, count_t, x_in, start_out, start_in, entry_out, entry_in,
    exit_out, exit_in, window_out, window_in,
    hop_send, hop_recv, pair_send, pair_recv, entry_send, entry_recv, exit_send, exit_recv,
    misc_send, misc_recv, x_send, x_recv, free_t, point_in, mate_aug,
):
    div, rem = lax.div, lax.rem
    f32, bf16 = jnp.float32, jnp.bfloat16
    row = lax.axis_index("row")
    col = lax.axis_index("col")
    peer = 1 - col
    devices = rows * 2
    paths = weight_ref.shape[1]
    share = paths // rows
    kept = paths // 2
    train = x_ref.shape[1]
    team = rows // 2
    own = train // team
    feat = freq_ref.shape[1]
    d_in = x_ref.shape[0]
    window = window_ref.shape[1]
    core = rem(row, 2)
    group = div(row, team)
    local = rem(row, team)
    flip = {"x": 2 - 4 * rem(div(row, 2), 2), "z": 4 - 8 * rem(div(row, 4), 2)}
    sibling = row + 1 - 2 * core
    block = 256

    def at(start, size, unit=None):
        return pl.ds(pl.multiple_of(start, unit or size), size)

    def mate(d):
        return rem(local + d + 1, team)

    def remote(src, dst, send, recv, device):
        return pltpu.make_async_remote_copy(
            src_ref=src, dst_ref=dst, send_sem=send, recv_sem=recv,
            device_id=device, device_id_type=MESH,
        )

    def loop(n, action):
        def one(i, carry):
            action(i)
            return carry

        lax.fori_loop(0, n, one, 0)

    def load(name):
        i = LOADS.index(name)
        src, dst = (
            (alpha_hbm, alpha_in), (x_hbm, x_ref), (index_hbm, index_ref),
            (target_hbm, target_ref), (noise_hbm, noise_ref), (velocity_hbm, velocity_in),
            (freq_hbm, freq_ref), (phase_hbm, phase_ref), (weight_hbm, weight_ref),
            (window_hbm, window_ref),
        )[i]
        return pltpu.make_async_copy(src, dst, load_sem.at[i])

    def loaded(*names):
        for name in names:
            load(name).wait()

    barrier = pltpu.get_barrier_semaphore()
    pl.semaphore_signal(barrier, inc=1, device_id=(row, peer), device_id_type=MESH)
    loop(team - 1, lambda d: pl.semaphore_signal(
        barrier, inc=1, device_id=(group * team + mate(d), col), device_id_type=MESH
    ))
    for name in LOADS:
        load(name).start()

    def source(mask):
        r = row
        for d in "xz":
            r = r + flip[d] if d in mask else r
        return r, (peer if "y" in mask else col)

    def first_row(r, c):
        return (c * team + rem(r, team)) * own

    def piece(step, mask, q, twin=False):
        r, c = source(mask)
        r = r + 1 - 2 * core if twin else r
        start, size, _ = pieces[q]
        return gathered.at[step, at(first_row(r, c) + start, size, 16), :]

    def hop(step, mask, d, q):
        ref = piece(step, mask, q)
        i = MASKS.index(mask_of(mask + d))
        return remote(
            ref, ref, hop_send.at[step, q, i], hop_recv.at[step, q, i], source(d)
        )

    def arrival(step, mask, q):
        ref = piece(step, mask, q)
        i = MASKS.index(mask)
        return remote(ref, ref, hop_send.at[step, q, i], hop_recv.at[step, q, i], (sibling, col))

    def pair(step, mask, q, twin=False):
        ref = piece(step, mask, q, twin)
        i = MASKS.index(mask) + 1 if mask else 0
        return remote(
            ref, ref, pair_send.at[step, q, i], pair_recv.at[step, q, i], (sibling, col)
        )

    count = range(len(pieces))

    def start_gather(step):
        for place in range(3):
            for q in count:
                hop(step, "", pieces[q][2][place], q).start()
        for q in count:
            pair(step, "", q).start()

    def relay(step, which):
        for q in count:
            order = pieces[q][2]
            mask = mask_of([order[i] for i in which])
            arrival(step, mask, q).wait_recv()
            for d in order[max(which) + 1 :]:
                hop(step, mask, d, q).start()
            pair(step, mask, q).start()

    def relay_first(step):
        for stage in range(3):
            relay(step, (stage,))

    def product(step, masks):
        for mask in masks:
            for q in count:
                pair(step, mask, q, True).wait_recv()
        wide = 2 * len(masks)
        r, c = source(masks[0])
        first = (c * team + div(rem(r, team), wide) * wide) * own
        span = at(first, wide * own)
        return dot(tile[:, span], gathered[step, span, :])

    def x_span(on_core, part):
        width = train // 4
        return at((on_core * 2 + part) * width, width)

    def x_copy(part):
        cols = x_span(core, part)
        return remote(
            x_ref.at[:, cols], x_in.at[:, cols], x_send.at[0, part], x_recv.at[0, part],
            (row, peer),
        )

    def x_pair(part, twin=False):
        ref = x_in.at[:, x_span(1 - core if twin else core, part)]
        return remote(ref, ref, x_send.at[1, part], x_recv.at[1, part], (sibling, col))

    def point_copy():
        return remote(
            x_ref.at[:, at(local * own, own)], point_in, x_send.at[2, 0], x_recv.at[2, 0],
            (row, peer),
        )

    def prior_copy():
        return remote(prior_out, prior_in, misc_send.at[2], misc_recv.at[2], (row, peer))

    parts = window_out.shape[0]

    def window_copy(part):
        return remote(
            window_out.at[part], window_in.at[part],
            misc_send.at[3 + part], misc_recv.at[3 + part], (row, peer),
        )

    def entry_refs(kind):
        if kind == 0:
            return start_out, start_in
        return entry_out.at[kind - 1], entry_in.at[kind - 1]

    def entry_copy(kind, d):
        m = mate(d)
        out, into = entry_refs(kind)
        return remote(
            out.at[:, at(m * own, own)], into.at[at(local * share, share), :],
            entry_send.at[kind, m], entry_recv.at[kind, local], (group * team + m, col),
        )

    def entry_arrival(kind, d):
        m = mate(d)
        out, into = entry_refs(kind)
        return remote(
            out.at[:, at(m * own, own)], into.at[at(m * share, share), :],
            entry_send.at[kind, m], entry_recv.at[kind, m], (group * team + m, col),
        )

    def send_entry(kind, value):
        out, into = entry_refs(kind)
        if kind:
            out[...] = value
        loop(team - 1, lambda d: entry_copy(kind, d).start())
        into[at(local * share, share), :] = out[:, at(local * own, own)]

    def take_entry(kind):
        loop(team - 1, lambda d: entry_arrival(kind, d).wait_recv())
        return entry_refs(kind)[1][...].astype(f32).T

    def exit_copy(kind, d):
        m = mate(d)
        return remote(
            exit_out.at[kind, at(m * share, share), :],
            exit_in.at[kind, :, at(local * own, own)],
            exit_send.at[kind, m], exit_recv.at[kind, local], (group * team + m, col),
        )

    def exit_arrival(kind, d):
        m = mate(d)
        return remote(
            exit_out.at[kind, at(m * share, share), :],
            exit_in.at[kind, :, at(m * own, own)],
            exit_send.at[kind, m], exit_recv.at[kind, m], (group * team + m, col),
        )

    def send_exit(kind, value):
        exit_out[kind] = value.T.astype(bf16)
        loop(team - 1, lambda d: exit_copy(kind, d).start())
        exit_in[kind, :, at(local * own, own)] = exit_out[kind, at(local * share, share), :]

    def take_exit(kind):
        loop(team - 1, lambda d: exit_arrival(kind, d).wait_recv())
        return exit_in[kind].astype(f32)

    def dot(a, b):
        return jnp.dot(a, b, preferred_element_type=f32)

    def against(a, b):
        return lax.dot_general(a, b, (((1,), (1,)), ((), ())), preferred_element_type=f32)

    def add_train(ref, c):
        def one(i):
            x = ref[:, at(i * block, block)]
            cols = at(c * train + i * block, block)
            for part in range(3):
                train_aug[part * d_in : (part + 1) * d_in, cols] = x
            norm = DIST_SCALE * jnp.sum(jnp.square(x.astype(f32)), axis=0, keepdims=True)
            tail = tail_rows([1.0, 1.0, 1.0] + split_three(norm), 16, block)
            train_aug[3 * d_in : 3 * d_in + 16, cols] = tail.astype(bf16)
            train_aug[3 * d_in + 16 :, cols] = jnp.zeros((d_in - 16, block), bf16)

        loop(train // block, one)

    def add_points():
        for i in range(own // block):
            x = x_ref[:, at(local * own + i * block, block)].astype(f32)
            norm = DIST_SCALE * jnp.sum(jnp.square(x), axis=0, keepdims=True)
            tail = tail_rows(split_three(norm) + [1.0, 1.0, 1.0], d_in, block)
            stack = jnp.concatenate(split_three(-2.0 * DIST_SCALE * x) + [tail], axis=0)
            point_aug[i * block : (i + 1) * block, :] = stack.T.astype(bf16)

    def add_window():
        for part in range(3):
            window_aug[part * d_in : (part + 1) * d_in, :] = window_ref[...]
        window_aug[3 * d_in :, :] = tail_rows([1.0] * 3, d_in, window).astype(bf16)

    def add_freq():
        def one(i):
            cols = at(i * block, block)
            tail = tail_rows(split_three(phase_ref[:, cols] * TURN), d_in, block)
            stack = jnp.concatenate(
                split_three(freq_ref[:, cols].astype(f32) * TURN) + [tail], axis=0
            )
            freq_t[cols, :] = stack.T.astype(bf16)
            weight_t[:, cols] = weight_ref[cols, :].astype(f32).T.astype(bf16)

        loop(feat // block, one)

    def count_points(step):
        lanes = 128
        width = index_ref.shape[1] // devices
        index = jnp.concatenate(
            [index_ref[step : step + 1, at((2 * i + col) * width, width)] for i in range(rows)],
            axis=1,
        )
        index = index - col * train
        high_ids = lax.broadcasted_iota(jnp.int32, (train // lanes, 1), 0)
        low_ids = lax.broadcasted_iota(jnp.int32, (lanes, 1), 0)
        high = ((index >> 7) == high_ids).astype(f32).astype(bf16)
        low = ((index & 127) == low_ids).astype(f32).astype(bf16)
        table = against(high, low)
        for i in range(train // lanes):
            count_ref[step : step + 1, i * lanes : (i + 1) * lanes] = table[i : i + 1, :]

    def spread_counts(step):
        line = count_ref[step : step + 1, at(local * own, own)]
        count_t[step] = jnp.broadcast_to(line, (kept, own)).T

    def sums_over_features(rhs, weights):
        phi_buf[...] = scaled_cos(dot(freq_t[...], rhs), scale_coeffs).astype(bf16)
        return dot(weights, phi_buf[...])

    def add_mate():
        for part in range(3):
            mate_aug[part * d_in : (part + 1) * d_in, :] = point_in[...]
        mate_aug[3 * d_in :, :] = tail_rows([1.0] * 3, d_in, own).astype(bf16)

    def prior_points(rhs, out):
        out[...] = sums_over_features(rhs, weight_t[at(group * kept, kept), :]).T

    def fill_tile(i):
        for part in range(2):
            cols = at(i * 4 * block + part * 2 * block, 2 * block)
            for half in range(2):
                span = slice(half * own // 2, (half + 1) * own // 2)
                dist_sq = jnp.maximum(dot(point_aug[span, :], train_aug[:, cols]), 1e-30)
                scaled = dist_sq * lax.rsqrt(dist_sq)
                tile[span, cols] = ((1.0 + scaled) * jnp.exp(-scaled)).astype(bf16)

    tiles = train // (4 * block)

    def fill_tiles(c, first, n):
        loop(n, lambda i: fill_tile(c * tiles + first + i))

    def window_work(i):
        width = window // parts
        span = slice(i * width, (i + 1) * width)
        total = sums_over_features(window_aug[:, span], weight_t[...])
        prior_ref[:, span] = jnp.where(col == 0, total[:kept], total[kept:])
        window_out[i] = jnp.where(col == 0, total[kept:], total[:kept]).astype(bf16)
        window_copy(i).start()

    loaded("alpha")
    start_out[...] = alpha_in[...].astype(bf16)
    loaded("x")
    add_points()
    pl.semaphore_wait(barrier, team)
    send_entry(0, None)
    point_copy().start()
    x_copy(0).start()
    add_train(x_ref, col)
    fill_tiles(col, 0, 1)
    loaded("index")
    count_points(0)
    count_points(1)
    gathered[0, at(first_row(row, col), own), :] = take_entry(0).astype(bf16)
    start_gather(0)
    x_copy(1).start()
    loaded("freq", "phase", "weight")
    add_freq()
    point_copy().wait_recv()
    add_mate()
    prior_points(mate_aug[...], prior_out)
    prior_copy().start()
    fill_tiles(col, 1, tiles - 1)
    relay_first(0)
    prior_points(train_aug[:, at(col * train + local * own, own)], prior_t)
    x_copy(0).wait_recv()
    x_pair(0).start()
    for step in range(steps - 1):
        spread_counts(step)
    loaded("window")
    add_window()
    x_copy(1).wait_recv()
    x_pair(1).start()
    loaded("target", "noise", "velocity")
    base = noise_ref[...] - target_ref[...]
    speed = velocity_in[...]
    free = alpha_in[...]
    frees = []
    for step in range(steps - 1):
        speed = MOMENTUM * speed - STEP_SIZE * (
            count_ref[step : step + 1, :] * (NOISE_VAR * free + base)
        )
        free = free + speed
        frees.append(free)
    alpha_ref[...] = free
    velocity_ref[...] = speed
    for part in (0, 1):
        x_pair(part, True).wait_recv()
    add_train(x_in, peer)
    fill_tiles(peer, 0, 1)
    relay(0, (0, 1))
    send_entry(1, frees[0])
    fill_tiles(peer, 1, 1)
    relay(0, (0, 2))
    relay(0, (1, 2))
    send_entry(2, frees[1])
    fill_tiles(peer, 2, tiles - 2)
    relay(0, (0, 1, 2))
    for mask in ("",) + MASKS:
        for q in count:
            pair(0, mask, q, True).wait_recv()
    acc[...] = dot(tile[...], gathered[0])
    prior_copy().wait_recv()
    prior_t[...] += prior_in[...]

    for step in range(1, steps + 1):
        sums = acc[...] + prior_t[...]
        if step == 1:
            speed = -STEP_SIZE * (count_t[0] * sums)
            pull = speed
        else:
            pull = pull_a[...]
            speed = MOMENTUM * pull_v[...] - STEP_SIZE * (
                count_t[step - 1] * (sums + NOISE_VAR * pull)
            )
            pull = pull + speed
        if step == steps:
            send_exit(1, speed)
            break
        pull_v[...] = speed
        pull_a[...] = pull
        free = take_entry(1) if step == 1 else free_t[...]
        gathered[step, at(first_row(row, col), own), :] = (free + pull).astype(bf16)
        start_gather(step)
        chunks = parts // (steps - 1)
        first = (step - 1) * chunks
        window_work(first)
        relay_first(step)
        for i in range(1, chunks):
            window_work(first + i)
        relay(step, (0, 1))
        acc[...] = product(step, ("",))
        if step == 1:
            count_points(steps - 1)
            spread_counts(steps - 1)
        acc[...] += product(step, ("x",))
        relay(step, (0, 2))
        relay(step, (1, 2))
        if step == steps - 1:
            send_exit(0, pull_a[...])
        acc[...] += product(step, ("y", "yx"))
        relay(step, (0, 1, 2))
        if step == 1:
            final = count_ref[steps - 1 : steps, :]
            base = noise_ref[...] - target_ref[...]
            velocity_ref[...] = MOMENTUM * velocity_ref[...] - STEP_SIZE * (
                final * (NOISE_VAR * alpha_ref[...] + base)
            )
            free_t[...] = take_entry(2)
        acc[...] += product(step, ("z", "xz"))
        acc[...] += product(step, ("yz",))
        acc[...] += product(step, ("yxz",))

    alpha_ref[...] += take_exit(0)
    for part in range(parts):
        window_copy(part).wait()
        width = window // parts
        span = slice(part * width, (part + 1) * width)
        prior_ref[:, span] = prior_ref[:, span] + window_in[part].astype(f32)
    speed = velocity_ref[...] + take_exit(1)
    velocity_ref[...] = speed
    alpha_ref[...] += speed
    for part in (0, 1):
        x_copy(part).wait_send()
        x_pair(part).wait_send()
    prior_copy().wait_send()
    point_copy().wait_send()
    for kind in range(steps):
        loop(team - 1, lambda d: entry_copy(kind, d).wait_send())
    for kind in range(2):
        loop(team - 1, lambda d: exit_copy(kind, d).wait_send())
    for step in range(steps):
        for q in count:
            for mask in MASKS:
                arrival(step, mask, q).wait_send()
                pair(step, mask, q).wait_send()
            pair(step, "", q).wait_send()


def fused_shards(
    x_train, targets, noise_draws, alpha_init, velocity_init, frequencies, phases, path_weights,
    x_window, batch_index,
):
    rows = lax.axis_size("row")
    col_count = lax.axis_size("col")
    d_in, train = x_train.shape
    steps = batch_index.shape[0]
    feat, paths = path_weights.shape
    share = paths // rows
    own = 2 * train // rows
    kept = paths // 2
    window = x_window.shape[1]
    parts = 4
    coeffs = sine_coeffs((2.0 / (feat * col_count)) ** 0.5)
    vmem = pl.BlockSpec(memory_space=pltpu.VMEM)
    dma = pltpu.SemaphoreType.DMA
    f32, bf16 = jnp.float32, jnp.bfloat16
    n = len(PIECES)
    alpha, velocity, prior = pl.pallas_call(
        functools.partial(fused_kernel, coeffs, steps, rows, PIECES),
        in_specs=[pl.BlockSpec(memory_space=pltpu.HBM)] * 10,
        out_specs=[vmem] * 3,
        out_shape=(
            jax.ShapeDtypeStruct((share, train), f32),
            jax.ShapeDtypeStruct((share, train), f32),
            jax.ShapeDtypeStruct((kept, window), f32),
        ),
        scratch_shapes=[
            pltpu.VMEM((d_in, train), bf16),
            pltpu.VMEM((1, train), f32),
            pltpu.VMEM((share, train), f32),
            pltpu.VMEM((share, train), f32),
            pltpu.VMEM((share, train), f32),
            pltpu.VMEM((d_in, feat), bf16),
            pltpu.VMEM((1, feat), f32),
            pltpu.VMEM((feat, paths), bf16),
            pltpu.VMEM((d_in, window), bf16),
            pltpu.VMEM(batch_index.shape, jnp.int32),
            dma((10,)),
            pltpu.VMEM((steps, 2 * train, kept), bf16),
            pltpu.VMEM((own, 2 * train), bf16),
            pltpu.VMEM((4 * d_in, 2 * train), bf16),
            pltpu.VMEM((4 * d_in, window), bf16),
            pltpu.VMEM((own, 4 * d_in), bf16),
            pltpu.VMEM((feat, 4 * d_in), bf16),
            pltpu.VMEM((paths, feat), bf16),
            pltpu.VMEM((feat, own), bf16),
            pltpu.VMEM((own, kept), f32),
            pltpu.VMEM((own, kept), f32),
            pltpu.VMEM((own, kept), f32),
            pltpu.VMEM((own, kept), f32),
            pltpu.VMEM((own, kept), f32),
            pltpu.VMEM((own, kept), f32),
            pltpu.VMEM((steps, train), f32),
            pltpu.VMEM((steps, own, kept), f32),
            pltpu.VMEM((d_in, train), bf16),
            pltpu.VMEM((share, train), bf16),
            pltpu.VMEM((kept, own), bf16),
            pltpu.VMEM((steps - 1, share, train), f32),
            pltpu.VMEM((steps - 1, kept, own), f32),
            pltpu.VMEM((2, kept, own), bf16),
            pltpu.VMEM((2, share, train), bf16),
            pltpu.VMEM((parts, kept, window // parts), bf16),
            pltpu.VMEM((parts, kept, window // parts), bf16),
            dma((steps, n, 7)), dma((steps, n, 7)), dma((steps, n, 8)), dma((steps, n, 8)),
            dma((steps, rows // 2)), dma((steps, rows // 2)),
            dma((2, rows // 2)), dma((2, rows // 2)),
            dma((3 + parts,)), dma((3 + parts,)), dma((3, 2)), dma((3, 2)),
            pltpu.VMEM((own, kept), f32),
            pltpu.VMEM((d_in, own), bf16),
            pltpu.VMEM((4 * d_in, own), bf16),
        ],
        compiler_params=pltpu.CompilerParams(
            collective_id=0, has_side_effects=True, vmem_limit_bytes=44 * 1024 * 1024
        ),
    )(
        *(pltpu.with_memory_space_constraint(a, pltpu.HBM) for a in (
            x_train, targets[None, :], noise_draws.T, alpha_init.T, velocity_init.T, frequencies,
            phases[None, :], path_weights, x_window, batch_index,
        ))
    )
    return alpha.T, velocity.T, prior


def fits(mesh, args):
    x_train, batch_index, path_weights, x_window = args[0], args[9], args[7], args[8]
    rows = mesh.shape["row"]
    d_in, train = x_train.shape
    feat, paths = path_weights.shape
    return (
        mesh.shape["col"] == 2 and rows == 16 and d_in == 64 and train == 256 * rows
        and paths == 16 * rows and feat % 1024 == 0 and x_window.shape[1] == 2048
        and batch_index.shape[0] == 3 and batch_index.shape[1] % (256 * rows) == 0
    )


def solution(mesh):
    def body(*args):
        return (fused_shards if fits(mesh, args) else shards)(*args)

    placed = (
        P(None, "col"),
        P("col"),
        P("col", "row"),
        P("col", "row"),
        P("col", "row"),
        P(None, "col"),
        P("col"),
        P("col", None),
        P(None, "row"),
        P(),
    )
    return jax.shard_map(
        body,
        mesh=mesh,
        in_specs=placed,
        out_specs=(P("col", "row"), P("col", "row"), P("col", "row")),
        check_vma=False,
    )
```

```python
import functools

import jax
import jax.numpy as jnp
import numpy as np
from jax import lax
from jax.experimental import pallas as pl
from jax.experimental.pallas import tpu as pltpu
from jax.sharding import PartitionSpec as P

SQRT_THREE = 1.7320508075688772
LENGTH = 1.15
NOISE_VAR = 0.25
MOMENTUM = 0.9
STEP_SIZE = 0.5


def sine_coeffs(scale):
    nodes = 4
    k = np.arange(nodes)
    v = (np.cos((2 * k + 1) * np.pi / (2 * nodes)) + 1) / 2 / 16
    z = np.sqrt(v)
    q = np.sin(2 * np.pi * z) / z
    return [float(c * scale) for c in np.linalg.solve(np.vander(v, nodes, increasing=True), q)]


def scaled_cos(turns, coeffs):
    z = 0.25 - jnp.abs(turns - jnp.round(turns))
    v = z * z
    q = coeffs[-1]
    for c in coeffs[-2::-1]:
        q = q * v + c
    return q * z


def prior_kernel(coeffs, tile_f, freq_ref, phase_ref, weight_ref, point_ref, out_ref):
    feat = freq_ref.shape[0]
    points = point_ref[...]

    def body(i, acc):
        rows = pl.ds(pl.multiple_of(i * tile_f, tile_f), tile_f)
        arg = jnp.dot(freq_ref[rows, :], points, preferred_element_type=jnp.float32)
        turns = (arg + phase_ref[rows, :]) * (0.5 / np.pi)
        phi = scaled_cos(turns, coeffs).astype(jnp.bfloat16)
        return acc + lax.dot_general(
            weight_ref[rows, :], phi, (((0,), (0,)), ((), ())), preferred_element_type=jnp.float32
        )

    out_ref[...] = lax.fori_loop(0, feat // tile_f, body, jnp.zeros(out_ref.shape, jnp.float32))


def prior_sums(freq_t, phase_col, weights, points, total_feat):
    feat, d_in = freq_t.shape
    paths = weights.shape[1]
    n = points.shape[1]
    tile_n = min(512, n)
    coeffs = sine_coeffs((2.0 / total_feat) ** 0.5)
    return pl.pallas_call(
        functools.partial(prior_kernel, coeffs, min(256, feat)),
        grid=(n // tile_n,),
        in_specs=[
            pl.BlockSpec((feat, d_in), lambda i: (0, 0)),
            pl.BlockSpec((feat, 1), lambda i: (0, 0)),
            pl.BlockSpec((feat, paths), lambda i: (0, 0)),
            pl.BlockSpec((d_in, tile_n), lambda i: (0, i)),
        ],
        out_specs=pl.BlockSpec((paths, tile_n), lambda i: (0, i)),
        out_shape=jax.ShapeDtypeStruct((paths, n), jnp.float32),
        cost_estimate=pl.CostEstimate(
            flops=2 * feat * n * (paths + d_in), bytes_accessed=4 * paths * n, transcendentals=feat * n
        ),
    )(freq_t, phase_col, weights, points)


def matern(points, train):
    inner = lax.dot_general(
        train, points, (((0,), (0,)), ((), ())), preferred_element_type=jnp.float32
    )
    point_norm = jnp.sum(jnp.square(points.astype(jnp.float32)), axis=0)
    train_norm = jnp.sum(jnp.square(train.astype(jnp.float32)), axis=0)
    dist_sq = jnp.maximum(train_norm[:, None] + point_norm[None, :] - 2.0 * inner, 0.0)
    scaled = SQRT_THREE / LENGTH * jnp.sqrt(dist_sq)
    return ((1.0 + scaled) * jnp.exp(-scaled)).astype(jnp.bfloat16)


def point_counts(index, start, count):
    lanes = 128
    local = index - start
    high = (local // lanes)[:, None, :] == lax.broadcasted_iota(
        jnp.int32, (1, count // lanes, 1), 1
    )
    low = (local % lanes)[:, None, :] == lax.broadcasted_iota(jnp.int32, (1, lanes, 1), 1)
    tables = lax.dot_general(
        high.astype(jnp.bfloat16),
        low.astype(jnp.bfloat16),
        (((2,), (2,)), ((0,), (0,))),
        preferred_element_type=jnp.float32,
    )
    return tables.reshape(index.shape[0], count)


def shards(
    x_train,
    targets,
    noise_draws,
    alpha_init,
    velocity_init,
    frequencies,
    phases,
    path_weights,
    x_window,
    batch_index,
):
    row_count = lax.axis_size("row")
    col_count = lax.axis_size("col")
    row_id = lax.axis_index("row")
    col_id = lax.axis_index("col")
    train_cols = x_train.shape[1]
    own = train_cols // row_count
    steps = batch_index.shape[0]
    total_feat = frequencies.shape[1] * col_count

    mine = lax.dynamic_slice_in_dim(x_train, row_id * own, own, 1)
    points = lax.all_gather(mine, "col", axis=1, tiled=True)
    freq_t = frequencies.T
    phase_col = phases[:, None]
    kernel_tile = matern(points, x_train)
    prior_rows = prior_sums(freq_t, phase_col, path_weights, points, total_feat)
    window = prior_sums(freq_t, phase_col, path_weights, x_window, total_feat)
    prior_window = lax.psum_scatter(window, "col", scatter_dimension=0, tiled=True)

    counts = point_counts(batch_index, col_id * train_cols, train_cols)
    base = (noise_draws - targets[:, None]).T
    dual, velocity = alpha_init.T, velocity_init.T
    for step in range(steps):
        coeffs = lax.all_gather(dual.astype(jnp.bfloat16), "row", axis=0, tiled=True)
        sums = jnp.dot(coeffs, kernel_tile, preferred_element_type=jnp.float32) + prior_rows
        mine_sums = lax.psum_scatter(sums, "col", scatter_dimension=1, tiled=True)
        arrived = lax.all_to_all(mine_sums, "row", split_axis=0, concat_axis=1, tiled=True)
        gradient = counts[step][None, :] * (arrived + NOISE_VAR * dual + base)
        velocity = MOMENTUM * velocity - STEP_SIZE * gradient
        dual = dual + velocity
    return (dual.T, velocity.T, prior_window)


MESH = pl.DeviceIdType.MESH
TURN = 1.0 / (2.0 * np.pi)
DIST_SCALE = 3.0 / (LENGTH * LENGTH)


def split_three(value):
    parts = []
    for _ in range(3):
        part = value.astype(jnp.bfloat16).astype(jnp.float32)
        parts.append(part)
        value = value - part
    return parts


def tail_rows(rows, count, n):
    at = lax.broadcasted_iota(jnp.int32, (count, n), 0)
    tail = jnp.zeros((count, n), jnp.float32)
    for i, row in enumerate(rows):
        tail = jnp.where(at == i, row, tail)
    return tail


DIMS = "yxz"
LOADS = (
    "alpha", "x", "index", "target", "noise", "velocity", "freq", "phase", "weight", "window",
)
ORDERS = ("yxz", "yzx", "yxz", "yzx")
MASKS = ("y", "x", "z", "yx", "yz", "xz", "yxz")


def mask_of(dims):
    return "".join(d for d in DIMS if d in dims)


def fused_kernel(
    scale_coeffs, steps, rows, pieces, x_hbm, target_hbm, noise_hbm, alpha_hbm, velocity_hbm,
    freq_hbm, phase_hbm, weight_hbm, window_hbm, index_hbm, alpha_ref, velocity_ref, prior_ref,
    x_ref, target_ref, noise_ref, alpha_in, velocity_in, freq_ref, phase_ref, weight_ref,
    window_ref, index_ref, load_sem,
    gathered, tile, train_aug, window_aug, point_aug, freq_t, weight_t, phi_buf, acc,
    pull_a, pull_v, prior_t, prior_out, prior_in, count_ref, count_t, x_in, start_out, start_in, entry_out, entry_in,
    exit_out, exit_in, window_out, window_in,
    hop_send, hop_recv, pair_send, pair_recv, entry_send, entry_recv, exit_send, exit_recv,
    misc_send, misc_recv, x_send, x_recv, free_t, point_in, mate_aug,
):
    div, rem = lax.div, lax.rem
    f32, bf16 = jnp.float32, jnp.bfloat16
    row = lax.axis_index("row")
    col = lax.axis_index("col")
    peer = 1 - col
    devices = rows * 2
    paths = weight_ref.shape[1]
    share = paths // rows
    kept = paths // 2
    train = x_ref.shape[1]
    team = rows // 2
    own = train // team
    feat = freq_ref.shape[1]
    d_in = x_ref.shape[0]
    window = window_ref.shape[1]
    core = rem(row, 2)
    group = div(row, team)
    local = rem(row, team)
    flip = {"x": 2 - 4 * rem(div(row, 2), 2), "z": 4 - 8 * rem(div(row, 4), 2)}
    sibling = row + 1 - 2 * core
    block = 256

    def at(start, size, unit=None):
        return pl.ds(pl.multiple_of(start, unit or size), size)

    def mate(d):
        return rem(local + d + 1, team)

    def remote(src, dst, send, recv, device):
        return pltpu.make_async_remote_copy(
            src_ref=src, dst_ref=dst, send_sem=send, recv_sem=recv,
            device_id=device, device_id_type=MESH,
        )

    def loop(n, action):
        def one(i, carry):
            action(i)
            return carry

        lax.fori_loop(0, n, one, 0)

    def load(name):
        i = LOADS.index(name)
        src, dst = (
            (alpha_hbm, alpha_in), (x_hbm, x_ref), (index_hbm, index_ref),
            (target_hbm, target_ref), (noise_hbm, noise_ref), (velocity_hbm, velocity_in),
            (freq_hbm, freq_ref), (phase_hbm, phase_ref), (weight_hbm, weight_ref),
            (window_hbm, window_ref),
        )[i]
        return pltpu.make_async_copy(src, dst, load_sem.at[i])

    def loaded(*names):
        for name in names:
            load(name).wait()

    barrier = pltpu.get_barrier_semaphore()
    pl.semaphore_signal(barrier, inc=1, device_id=(row, peer), device_id_type=MESH)
    loop(team - 1, lambda d: pl.semaphore_signal(
        barrier, inc=1, device_id=(group * team + mate(d), col), device_id_type=MESH
    ))
    for name in LOADS:
        load(name).start()

    def source(mask):
        r = row
        for d in "xz":
            r = r + flip[d] if d in mask else r
        return r, (peer if "y" in mask else col)

    def first_row(r, c):
        return (c * team + rem(r, team)) * own

    def piece(step, mask, q, twin=False):
        r, c = source(mask)
        r = r + 1 - 2 * core if twin else r
        start, size, _ = pieces[q]
        return gathered.at[step, at(first_row(r, c) + start, size, 16), :]

    def hop(step, mask, d, q):
        ref = piece(step, mask, q)
        i = MASKS.index(mask_of(mask + d))
        return remote(
            ref, ref, hop_send.at[step, q, i], hop_recv.at[step, q, i], source(d)
        )

    def arrival(step, mask, q):
        ref = piece(step, mask, q)
        i = MASKS.index(mask)
        return remote(ref, ref, hop_send.at[step, q, i], hop_recv.at[step, q, i], (sibling, col))

    def pair(step, mask, q, twin=False):
        ref = piece(step, mask, q, twin)
        i = MASKS.index(mask) + 1 if mask else 0
        return remote(
            ref, ref, pair_send.at[step, q, i], pair_recv.at[step, q, i], (sibling, col)
        )

    count = range(len(pieces))

    def start_gather(step):
        for place in range(3):
            for q in count:
                hop(step, "", pieces[q][2][place], q).start()
        for q in count:
            pair(step, "", q).start()

    def relay(step, which):
        for q in count:
            order = pieces[q][2]
            mask = mask_of([order[i] for i in which])
            arrival(step, mask, q).wait_recv()
            for d in order[max(which) + 1 :]:
                hop(step, mask, d, q).start()
            pair(step, mask, q).start()

    def relay_first(step):
        for stage in range(3):
            relay(step, (stage,))

    def product(step, masks):
        for mask in masks:
            for q in count:
                pair(step, mask, q, True).wait_recv()
        wide = 2 * len(masks)
        r, c = source(masks[0])
        first = (c * team + div(rem(r, team), wide) * wide) * own
        span = at(first, wide * own)
        return dot(tile[:, span], gathered[step, span, :])

    def x_span(on_core, part):
        width = train // 4
        return at((on_core * 2 + part) * width, width)

    def x_copy(part):
        cols = x_span(core, part)
        return remote(
            x_ref.at[:, cols], x_in.at[:, cols], x_send.at[0, part], x_recv.at[0, part],
            (row, peer),
        )

    def x_pair(part, twin=False):
        ref = x_in.at[:, x_span(1 - core if twin else core, part)]
        return remote(ref, ref, x_send.at[1, part], x_recv.at[1, part], (sibling, col))

    def point_copy():
        return remote(
            x_ref.at[:, at(local * own, own)], point_in, x_send.at[2, 0], x_recv.at[2, 0],
            (row, peer),
        )

    def prior_copy():
        return remote(prior_out, prior_in, misc_send.at[2], misc_recv.at[2], (row, peer))

    parts = window_out.shape[0]

    def window_copy(part):
        return remote(
            window_out.at[part], window_in.at[part],
            misc_send.at[3 + part], misc_recv.at[3 + part], (row, peer),
        )

    def entry_refs(kind):
        if kind == 0:
            return start_out, start_in
        return entry_out.at[kind - 1], entry_in.at[kind - 1]

    def entry_copy(kind, d):
        m = mate(d)
        out, into = entry_refs(kind)
        return remote(
            out.at[:, at(m * own, own)], into.at[at(local * share, share), :],
            entry_send.at[kind, m], entry_recv.at[kind, local], (group * team + m, col),
        )

    def entry_arrival(kind, d):
        m = mate(d)
        out, into = entry_refs(kind)
        return remote(
            out.at[:, at(m * own, own)], into.at[at(m * share, share), :],
            entry_send.at[kind, m], entry_recv.at[kind, m], (group * team + m, col),
        )

    def send_entry(kind, value):
        out, into = entry_refs(kind)
        if kind:
            out[...] = value
        loop(team - 1, lambda d: entry_copy(kind, d).start())
        into[at(local * share, share), :] = out[:, at(local * own, own)]

    def take_entry(kind):
        loop(team - 1, lambda d: entry_arrival(kind, d).wait_recv())
        return entry_refs(kind)[1][...].astype(f32).T

    def exit_copy(kind, d):
        m = mate(d)
        return remote(
            exit_out.at[kind, at(m * share, share), :],
            exit_in.at[kind, :, at(local * own, own)],
            exit_send.at[kind, m], exit_recv.at[kind, local], (group * team + m, col),
        )

    def exit_arrival(kind, d):
        m = mate(d)
        return remote(
            exit_out.at[kind, at(m * share, share), :],
            exit_in.at[kind, :, at(m * own, own)],
            exit_send.at[kind, m], exit_recv.at[kind, m], (group * team + m, col),
        )

    def send_exit(kind, value):
        exit_out[kind] = value.T.astype(bf16)
        loop(team - 1, lambda d: exit_copy(kind, d).start())
        exit_in[kind, :, at(local * own, own)] = exit_out[kind, at(local * share, share), :]

    def take_exit(kind):
        loop(team - 1, lambda d: exit_arrival(kind, d).wait_recv())
        return exit_in[kind].astype(f32)

    def dot(a, b):
        return jnp.dot(a, b, preferred_element_type=f32)

    def against(a, b):
        return lax.dot_general(a, b, (((1,), (1,)), ((), ())), preferred_element_type=f32)

    def add_train(ref, c):
        def one(i):
            x = ref[:, at(i * block, block)]
            cols = at(c * train + i * block, block)
            for part in range(3):
                train_aug[part * d_in : (part + 1) * d_in, cols] = x
            norm = DIST_SCALE * jnp.sum(jnp.square(x.astype(f32)), axis=0, keepdims=True)
            tail = tail_rows([1.0, 1.0, 1.0] + split_three(norm), 16, block)
            train_aug[3 * d_in : 3 * d_in + 16, cols] = tail.astype(bf16)
            train_aug[3 * d_in + 16 :, cols] = jnp.zeros((d_in - 16, block), bf16)

        loop(train // block, one)

    def add_points():
        for i in range(own // block):
            x = x_ref[:, at(local * own + i * block, block)].astype(f32)
            norm = DIST_SCALE * jnp.sum(jnp.square(x), axis=0, keepdims=True)
            tail = tail_rows(split_three(norm) + [1.0, 1.0, 1.0], d_in, block)
            stack = jnp.concatenate(split_three(-2.0 * DIST_SCALE * x) + [tail], axis=0)
            point_aug[i * block : (i + 1) * block, :] = stack.T.astype(bf16)

    def add_window():
        for part in range(3):
            window_aug[part * d_in : (part + 1) * d_in, :] = window_ref[...]
        window_aug[3 * d_in :, :] = tail_rows([1.0] * 3, d_in, window).astype(bf16)

    def add_freq():
        def one(i):
            cols = at(i * block, block)
            tail = tail_rows(split_three(phase_ref[:, cols] * TURN), d_in, block)
            stack = jnp.concatenate(
                split_three(freq_ref[:, cols].astype(f32) * TURN) + [tail], axis=0
            )
            freq_t[cols, :] = stack.T.astype(bf16)
            weight_t[:, cols] = weight_ref[cols, :].astype(f32).T.astype(bf16)

        loop(feat // block, one)

    def count_points(step):
        lanes = 128
        width = index_ref.shape[1] // devices
        index = jnp.concatenate(
            [index_ref[step : step + 1, at((2 * i + col) * width, width)] for i in range(rows)],
            axis=1,
        )
        index = index - col * train
        high_ids = lax.broadcasted_iota(jnp.int32, (train // lanes, 1), 0)
        low_ids = lax.broadcasted_iota(jnp.int32, (lanes, 1), 0)
        high = ((index >> 7) == high_ids).astype(f32).astype(bf16)
        low = ((index & 127) == low_ids).astype(f32).astype(bf16)
        table = against(high, low)
        for i in range(train // lanes):
            count_ref[step : step + 1, i * lanes : (i + 1) * lanes] = table[i : i + 1, :]

    def spread_counts(step):
        line = count_ref[step : step + 1, at(local * own, own)]
        count_t[step] = jnp.broadcast_to(line, (kept, own)).T

    def sums_over_features(rhs, weights):
        phi_buf[...] = scaled_cos(dot(freq_t[...], rhs), scale_coeffs).astype(bf16)
        return dot(weights, phi_buf[...])

    def add_mate():
        for part in range(3):
            mate_aug[part * d_in : (part + 1) * d_in, :] = point_in[...]
        mate_aug[3 * d_in :, :] = tail_rows([1.0] * 3, d_in, own).astype(bf16)

    def prior_points(rhs, out):
        out[...] = sums_over_features(rhs, weight_t[at(group * kept, kept), :]).T

    def fill_tile(i):
        for part in range(2):
            cols = at(i * 4 * block + part * 2 * block, 2 * block)
            for half in range(2):
                span = slice(half * own // 2, (half + 1) * own // 2)
                dist_sq = jnp.maximum(dot(point_aug[span, :], train_aug[:, cols]), 1e-30)
                scaled = dist_sq * lax.rsqrt(dist_sq)
                tile[span, cols] = ((1.0 + scaled) * jnp.exp(-scaled)).astype(bf16)

    tiles = train // (4 * block)

    def fill_tiles(c, first, n):
        loop(n, lambda i: fill_tile(c * tiles + first + i))

    def window_work(i):
        width = window // parts
        span = slice(i * width, (i + 1) * width)
        total = sums_over_features(window_aug[:, span], weight_t[...])
        prior_ref[:, span] = jnp.where(col == 0, total[:kept], total[kept:])
        window_out[i] = jnp.where(col == 0, total[kept:], total[:kept]).astype(bf16)
        window_copy(i).start()

    loaded("alpha")
    start_out[...] = alpha_in[...].astype(bf16)
    loaded("x")
    add_points()
    pl.semaphore_wait(barrier, team)
    send_entry(0, None)
    point_copy().start()
    x_copy(0).start()
    add_train(x_ref, col)
    fill_tiles(col, 0, 1)
    loaded("index")
    count_points(0)
    count_points(1)
    gathered[0, at(first_row(row, col), own), :] = take_entry(0).astype(bf16)
    start_gather(0)
    x_copy(1).start()
    loaded("freq", "phase", "weight")
    add_freq()
    point_copy().wait_recv()
    add_mate()
    prior_points(mate_aug[...], prior_out)
    prior_copy().start()
    fill_tiles(col, 1, tiles - 1)
    relay_first(0)
    loaded("target", "noise", "velocity")
    base = noise_ref[...] - target_ref[...]
    speed = velocity_in[...]
    free = alpha_in[...]
    frees = []
    for step in range(steps - 1):
        speed = MOMENTUM * speed - STEP_SIZE * (
            count_ref[step : step + 1, :] * (NOISE_VAR * free + base)
        )
        free = free + speed
        frees.append(free)
    alpha_ref[...] = free
    velocity_ref[...] = speed
    send_entry(1, frees[0])
    prior_points(train_aug[:, at(col * train + local * own, own)], prior_t)
    x_copy(0).wait_recv()
    x_pair(0).start()
    for step in range(steps - 1):
        spread_counts(step)
    loaded("window")
    add_window()
    x_copy(1).wait_recv()
    x_pair(1).start()
    for part in (0, 1):
        x_pair(part, True).wait_recv()
    add_train(x_in, peer)
    fill_tiles(peer, 0, 1)
    relay(0, (0, 1))
    fill_tiles(peer, 1, 1)
    relay(0, (0, 2))
    relay(0, (1, 2))
    send_entry(2, frees[1])
    fill_tiles(peer, 2, tiles - 2)
    relay(0, (0, 1, 2))
    for mask in ("",) + MASKS:
        for q in count:
            pair(0, mask, q, True).wait_recv()
    acc[...] = dot(tile[...], gathered[0])
    prior_copy().wait_recv()
    prior_t[...] += prior_in[...]

    for step in range(1, steps + 1):
        sums = acc[...] + prior_t[...]
        if step == 1:
            speed = -STEP_SIZE * (count_t[0] * sums)
            pull = speed
        else:
            pull = pull_a[...]
            speed = MOMENTUM * pull_v[...] - STEP_SIZE * (
                count_t[step - 1] * (sums + NOISE_VAR * pull)
            )
            pull = pull + speed
        if step == steps:
            send_exit(1, speed)
            break
        pull_v[...] = speed
        pull_a[...] = pull
        free = take_entry(1) if step == 1 else free_t[...]
        gathered[step, at(first_row(row, col), own), :] = (free + pull).astype(bf16)
        start_gather(step)
        chunks = parts // (steps - 1)
        first = (step - 1) * chunks
        window_work(first)
        relay_first(step)
        for i in range(1, chunks):
            window_work(first + i)
        relay(step, (0, 1))
        acc[...] = product(step, ("",))
        if step == 1:
            count_points(steps - 1)
            spread_counts(steps - 1)
        acc[...] += product(step, ("x",))
        relay(step, (0, 2))
        relay(step, (1, 2))
        if step == steps - 1:
            send_exit(0, pull_a[...])
        acc[...] += product(step, ("y", "yx"))
        relay(step, (0, 1, 2))
        if step == 1:
            final = count_ref[steps - 1 : steps, :]
            base = noise_ref[...] - target_ref[...]
            velocity_ref[...] = MOMENTUM * velocity_ref[...] - STEP_SIZE * (
                final * (NOISE_VAR * alpha_ref[...] + base)
            )
            free_t[...] = take_entry(2)
        acc[...] += product(step, ("z", "xz"))
        acc[...] += product(step, ("yz",))
        acc[...] += product(step, ("yxz",))

    alpha_ref[...] += take_exit(0)
    for part in range(parts):
        window_copy(part).wait()
        width = window // parts
        span = slice(part * width, (part + 1) * width)
        prior_ref[:, span] = prior_ref[:, span] + window_in[part].astype(f32)
    speed = velocity_ref[...] + take_exit(1)
    velocity_ref[...] = speed
    alpha_ref[...] += speed
    for part in (0, 1):
        x_copy(part).wait_send()
        x_pair(part).wait_send()
    prior_copy().wait_send()
    point_copy().wait_send()
    for kind in range(steps):
        loop(team - 1, lambda d: entry_copy(kind, d).wait_send())
    for kind in range(2):
        loop(team - 1, lambda d: exit_copy(kind, d).wait_send())
    for step in range(steps):
        for q in count:
            for mask in MASKS:
                arrival(step, mask, q).wait_send()
                pair(step, mask, q).wait_send()
            pair(step, "", q).wait_send()


def fused_shards(
    x_train, targets, noise_draws, alpha_init, velocity_init, frequencies, phases, path_weights,
    x_window, batch_index,
):
    rows = lax.axis_size("row")
    col_count = lax.axis_size("col")
    d_in, train = x_train.shape
    steps = batch_index.shape[0]
    feat, paths = path_weights.shape
    share = paths // rows
    own = 2 * train // rows
    kept = paths // 2
    window = x_window.shape[1]
    parts = 4
    coeffs = sine_coeffs((2.0 / (feat * col_count)) ** 0.5)
    vmem = pl.BlockSpec(memory_space=pltpu.VMEM)
    dma = pltpu.SemaphoreType.DMA
    f32, bf16 = jnp.float32, jnp.bfloat16
    n = len(ORDERS)
    pieces = tuple((i * (own // n), own // n, order) for i, order in enumerate(ORDERS))
    alpha, velocity, prior = pl.pallas_call(
        functools.partial(fused_kernel, coeffs, steps, rows, pieces),
        in_specs=[pl.BlockSpec(memory_space=pltpu.HBM)] * 10,
        out_specs=[vmem] * 3,
        out_shape=(
            jax.ShapeDtypeStruct((share, train), f32),
            jax.ShapeDtypeStruct((share, train), f32),
            jax.ShapeDtypeStruct((kept, window), f32),
        ),
        scratch_shapes=[
            pltpu.VMEM((d_in, train), bf16),
            pltpu.VMEM((1, train), f32),
            pltpu.VMEM((share, train), f32),
            pltpu.VMEM((share, train), f32),
            pltpu.VMEM((share, train), f32),
            pltpu.VMEM((d_in, feat), bf16),
            pltpu.VMEM((1, feat), f32),
            pltpu.VMEM((feat, paths), bf16),
            pltpu.VMEM((d_in, window), bf16),
            pltpu.VMEM(batch_index.shape, jnp.int32),
            dma((10,)),
            pltpu.VMEM((steps, 2 * train, kept), bf16),
            pltpu.VMEM((own, 2 * train), bf16),
            pltpu.VMEM((4 * d_in, 2 * train), bf16),
            pltpu.VMEM((4 * d_in, window), bf16),
            pltpu.VMEM((own, 4 * d_in), bf16),
            pltpu.VMEM((feat, 4 * d_in), bf16),
            pltpu.VMEM((paths, feat), bf16),
            pltpu.VMEM((feat, own), bf16),
            pltpu.VMEM((own, kept), f32),
            pltpu.VMEM((own, kept), f32),
            pltpu.VMEM((own, kept), f32),
            pltpu.VMEM((own, kept), f32),
            pltpu.VMEM((own, kept), f32),
            pltpu.VMEM((own, kept), f32),
            pltpu.VMEM((steps, train), f32),
            pltpu.VMEM((steps, own, kept), f32),
            pltpu.VMEM((d_in, train), bf16),
            pltpu.VMEM((share, train), bf16),
            pltpu.VMEM((kept, own), bf16),
            pltpu.VMEM((steps - 1, share, train), f32),
            pltpu.VMEM((steps - 1, kept, own), f32),
            pltpu.VMEM((2, kept, own), bf16),
            pltpu.VMEM((2, share, train), bf16),
            pltpu.VMEM((parts, kept, window // parts), bf16),
            pltpu.VMEM((parts, kept, window // parts), bf16),
            dma((steps, n, 7)), dma((steps, n, 7)), dma((steps, n, 8)), dma((steps, n, 8)),
            dma((steps, rows // 2)), dma((steps, rows // 2)),
            dma((2, rows // 2)), dma((2, rows // 2)),
            dma((3 + parts,)), dma((3 + parts,)), dma((3, 2)), dma((3, 2)),
            pltpu.VMEM((own, kept), f32),
            pltpu.VMEM((d_in, own), bf16),
            pltpu.VMEM((4 * d_in, own), bf16),
        ],
        compiler_params=pltpu.CompilerParams(
            collective_id=0, has_side_effects=True, vmem_limit_bytes=44 * 1024 * 1024
        ),
    )(
        *(pltpu.with_memory_space_constraint(a, pltpu.HBM) for a in (
            x_train, targets[None, :], noise_draws.T, alpha_init.T, velocity_init.T, frequencies,
            phases[None, :], path_weights, x_window, batch_index,
        ))
    )
    return alpha.T, velocity.T, prior


def fits(mesh, args):
    x_train, batch_index, path_weights, x_window = args[0], args[9], args[7], args[8]
    rows, cols = mesh.shape["row"], mesh.shape["col"]
    d_in, train = x_train.shape
    feat, paths = path_weights.shape
    steps, batch = batch_index.shape
    own = 2 * train // rows
    return (
        (rows, cols, steps) == (16, 2, 3) and d_in % 32 == 0 and train % 1024 == 0
        and own % 512 == 0 and paths % (16 * rows) == 0 and feat % 256 == 0
        and x_window.shape[1] == 4 * own and batch % (128 * rows * cols) == 0
    )


def solution(mesh):
    def body(*args):
        return (fused_shards if fits(mesh, args) else shards)(*args)

    placed = (
        P(None, "col"),
        P("col"),
        P("col", "row"),
        P("col", "row"),
        P("col", "row"),
        P(None, "col"),
        P("col"),
        P("col", None),
        P(None, "row"),
        P(),
    )
    return jax.shard_map(
        body,
        mesh=mesh,
        in_specs=placed,
        out_specs=(P("col", "row"), P("col", "row"), P("col", "row")),
        check_vma=False,
    )
```
